128 devices in a mesh: row: 16 (over z_hi, x, core), col: 8 (over y, z_lo).
Axes of the slice: x: 4, y: 4, z: 4 (z_hi: 2, z_lo: 2; z = z_hi * 2 + z_lo), core: 2. Of those that a mesh axis runs over, the one named last changes fastest.
Arguments:
- a_blocks: bfloat16 [128, 128, 9216], P('row', 'col'), may hold values from -0.625 to 0.625
- a_mask: int32 [128, 128], P('row', 'col'), may hold values from 0 to 1, as said below
- p_blocks: bfloat16 [128, 64, 9216], P('row', 'col'), may hold values from -3 to 3
- p_mask: int32 [128, 64], P('row', 'col'), may hold values from 0 to 1, as said below
- section_owner: int32 [2], replicated, may hold values from 0 to 7, as said below
- agg_order: int32 [64], replicated, may hold values from 0 to 63, as said below
Outputs:
- coarse: float32 [6144, 6144], P(('row', 'col'))
The draws below stay inside these ranges and needn't reach their ends.
Inputs may be any that keep to these rules, and one draw needn't show every extreme that they name: `a_mask`: each tile of 8 x 16 blocks (the fine block rows of one index of row and the fine block columns of one index of col) holds between 32 and 96 ones, and in every index of row some tile holds exactly 96. `section_owner`: distinct indices of col; one of the sections takes index 7. `agg_order`: each coarse block once. `p_mask`: with c = i // 2: fine block row i feeds aggregate agg_order[c] always, agg_order[c - 1] and agg_order[c + 1] possibly, agg_order[(c + 32) mod 64] always where i is a multiple of 2, aggregate ((i // 16 + 8 // 2) mod 8) * 8 + (i mod 8) always, and nothing else.
All inputs are finite; a program needn't handle non-finite values.
Results may differ from the reference program's by a relative error of at most 0.0029.
Values may be sent and summed in bfloat16 or wider, within the bound.
No kernel may reach another device: no remote copies, remote signals or barrier semaphores. Data moves between devices by JAX's collectives and lax.ppermute only.
A program may use at most 128 MiB of HBM per device.

```python
import jax
import jax.numpy as jnp
from jax import lax

BS = 96
BR = 8
CB = 8
SECTIONS = 2
NB = 128
NCB = 64
BK = 16
NZMAX = 96
N_ROW = 16
N_COL = 8


def aggregate_order(key):
    return jax.random.permutation(jax.random.fold_in(key, 7), NCB).astype(jnp.int32)


def draw_a_mask(key, part):
    cells = BR * BK
    count_key, column_key, order_key = jax.random.split(key, 3)
    tile_counts = jax.random.randint(count_key, (N_ROW, N_COL), cells // 4, NZMAX + 1)
    full_column = jax.random.randint(column_key, (N_ROW,), 0, N_COL)
    tile_counts = jnp.where(jnp.arange(N_COL)[None, :] == full_column[:, None], NZMAX, tile_counts)
    tile_keys = jax.random.split(order_key, N_ROW * N_COL)
    rank_table = jax.vmap(lambda one_key: jax.random.permutation(one_key, cells))(tile_keys)
    rank_table = rank_table.reshape(N_ROW, N_COL, BR, BK)
    chosen = rank_table < tile_counts[:, :, None, None]
    return chosen.astype(jnp.int32).transpose(0, 2, 1, 3).reshape(NB, NB)


def draw_agg_order(key, part):
    return aggregate_order(key)


def draw_p_mask(key, part):
    ordering = aggregate_order(key)
    ratio = NB // NCB
    fine_index = jnp.arange(NB)
    center = (fine_index // ratio)[:, None]
    coins = jax.random.randint(jax.random.fold_in(key, 11), (NB, 2), 0, 2)
    places = jnp.arange(NCB)[None, :]
    within = places == center
    within = within | (places == center - 1) & (coins[:, 0:1] == 1)
    within = within | (places == center + 1) & (coins[:, 1:2] == 1)
    far_place = (center + NCB // 2) % NCB
    within = within | (places == far_place) & (fine_index % ratio == 0)[:, None]
    inverse = jnp.zeros((NCB,), jnp.int32).at[ordering].set(jnp.arange(NCB, dtype=jnp.int32))
    linked = within[:, inverse]
    cross_col = (fine_index // BK + N_COL // 2) % N_COL * CB + fine_index % CB
    linked = linked | (places == cross_col[:, None])
    return linked.astype(jnp.int32)


def draw_section_owner(key, part):
    others_key, place_key = jax.random.split(jax.random.fold_in(key, 23))
    others = jax.random.permutation(others_key, N_COL - 1)[:SECTIONS - 1].astype(jnp.int32)
    listed = jnp.concatenate([jnp.full((1,), N_COL - 1, jnp.int32), others])
    spots = jax.random.permutation(place_key, SECTIONS)
    return listed[spots].astype(jnp.int32)


def levels(stream_key, dims, cuts, low, largest):
    level, own = 1.0, jax.random.fold_in(stream_key, 6)
    for position, shards_of in cuts:
        draws = jnp.exp(jax.random.uniform(jax.random.fold_in(own, position), (shards_of,), jnp.float32, low / len(cuts), largest / len(cuts)))
        level = level * jnp.repeat(draws, dims[position] // shards_of).reshape([-1 if axis == position else 1 for axis in range(len(dims))])
    return level


def centred(stream_key, dims, width, bound, pieces=(), kind=jnp.bfloat16):
    values = jax.random.normal(stream_key, dims, jnp.float32) * width
    if len(pieces) > 0:
        values = levels(stream_key, dims, pieces, -0.22, 0.18) * values
    return jnp.clip(values, min=-bound, max=bound).astype(kind)


def setup_inputs(seed: int = 0) -> dict:
    arg_keys = jax.random.split(jax.random.key(seed), 7)
    a_blocks = centred(arg_keys[0], (NB, NB, BS * BS), BS ** -0.5, 0.625, ((0, 16), (1, 8)))
    a_mask = draw_a_mask(jax.random.fold_in(arg_keys[6], 71), 0)
    p_blocks = centred(arg_keys[2], (NB, NCB, BS * BS), ((2.0 * (NB // NCB) * (NB // NCB) * BS) ** -0.25), 3.0, ((0, 16), (1, 8)))
    p_mask = draw_p_mask(jax.random.fold_in(arg_keys[6], 71), 0)
    section_owner = draw_section_owner(jax.random.fold_in(arg_keys[6], 71), 0)
    agg_order = draw_agg_order(jax.random.fold_in(arg_keys[6], 71), 0)
    return dict(a_blocks=a_blocks, a_mask=a_mask, p_blocks=p_blocks, p_mask=p_mask, section_owner=section_owner, agg_order=agg_order)


def reference(a_blocks, a_mask, p_blocks, p_mask, section_owner, agg_order):
    fine_operator = a_blocks * a_mask[:, :, None].astype(jnp.bfloat16)
    prolongation = p_blocks * p_mask[:, :, None].astype(jnp.bfloat16)
    prolong_four = prolongation.reshape(NB, NCB, BS, BS).astype(jnp.float32)
    product = jnp.zeros((NB, BS, NCB, BS), jnp.float32)
    for section_num in range(SECTIONS):
        offset = (section_owner[section_num] * BK).astype(jnp.int32)
        operator_panel = lax.dynamic_slice_in_dim(fine_operator, offset, BK, 1)
        operator_panel = operator_panel.reshape(NB, BK, BS, BS).astype(jnp.float32)
        prolong_panel = lax.dynamic_slice_in_dim(prolong_four, offset, BK, 0)
        product = product + jnp.einsum("ikab,kjbc->iajc", operator_panel, prolong_panel)
    fine_coarse = product.reshape(NB, BS, NCB * BS).astype(jnp.bfloat16)
    fine_coarse = lax.optimization_barrier(fine_coarse).astype(jnp.float32)
    coarse_full = jnp.einsum("iIab,iaj->Ibj", prolong_four, fine_coarse)
    return coarse_full[agg_order].reshape(NCB * BS, NCB * BS)
```

```python
import jax
import jax.numpy as jnp
from jax import lax
from jax.experimental import pallas as pl
from jax.experimental.pallas import tpu as pltpu
from jax.sharding import PartitionSpec as P

BS = 96
BR = 8
NCB = 64
KK = 4
WIDE = KK * BS
ROWS = 16
COLS = 8
PIECE = BS // ROWS
SLOTS = 16
LANES = PIECE * WIDE
USLOTS = 5
PW = 512
OUTSLOTS = 18
F32 = jnp.float32
BF16 = jnp.bfloat16


def lookup(table, index):
    hit = index[..., None] == jnp.arange(table.shape[0], dtype=jnp.int32)
    return jnp.sum(jnp.where(hit, table, 0), axis=-1)


def band_columns(rows, agg_order):
    center = rows // 2
    places = jnp.stack(
        [(center + NCB - 1) % NCB, center, (center + 1) % NCB, (center + NCB // 2) % NCB], axis=-1
    )
    return lookup(agg_order, places)


def partial_kernel(p_ref, mine_ref, a_ref, x_ref, own_ref, scr):
    seen = set()
    for i in range(BR):
        q = lax.dot_general(
            p_ref[i], a_ref[i], (((0,), (0,)), ((), ())), preferred_element_type=F32
        )
        local = i // 2
        for u in range(3):
            w = local + u
            value = q[u * BS : (u + 1) * BS]
            ref, at = (scr, 0) if w == 0 else (scr, 1) if w == 5 else (own_ref, w - 1)
            if w in seen:
                ref[at] += value
            else:
                ref[at] = value
                seen.add(w)
        if i % 2 == 0:
            scr[2 + local] = q[3 * BS : 4 * BS]
        scr[6 + i] = q[4 * BS : 5 * BS]
    mine = mine_ref[...].astype(F32)
    scr[14] = mine[:, :WIDE]
    scr[15, :, : PW - WIDE] = mine[:, WIDE:]
    scr[15, :, PW - WIDE :] = jnp.zeros((BS, 2 * WIDE - PW), F32)
    for octet in range(BS // 8):
        chunk = jnp.swapaxes(scr[:, octet * 8 : octet * 8 + 8, :], 0, 1)
        for e in range(8):
            j, pp = divmod(octet * 8 + e, PIECE)
            x_ref[j, :, pp * WIDE : (pp + 1) * WIDE] = chunk[e].astype(BF16)


def product_kernel(r_ref, own_ref, x_ref, scr, held):
    for octet in range(BS // 8):
        rows = []
        for e in range(8):
            j, pp = divmod(octet * 8 + e, PIECE)
            rows.append(r_ref[j, :, pp * WIDE : (pp + 1) * WIDE].astype(F32))
        scr[:, octet * 8 : octet * 8 + 8, :] = jnp.swapaxes(jnp.stack(rows), 0, 1)
    for kk in range(KK):
        right = jnp.concatenate([scr[8 + 2 * kk], scr[9 + 2 * kk][:, :BS]], axis=1).astype(BF16)
        for t in range(4):
            g = (own_ref[t] + scr[t] + scr[4 + t])[:, kk * BS : (kk + 1) * BS]
            high = g.astype(BF16)
            low = (g - high.astype(F32)).astype(BF16)
            out = jnp.dot(high, right, preferred_element_type=F32)
            out = out + jnp.dot(low, right, preferred_element_type=F32)
            span = slice(t * BS, (t + 1) * BS)
            x_ref[span, kk * WIDE : (kk + 1) * WIDE] = out[:, :WIDE].astype(BF16)
            if kk % 2 == 0:
                held[t] = out[:, WIDE:]
            else:
                sec = kk // 2
                cross = held[t] + out[:, WIDE:]
                x_ref[span, 4 * WIDE + sec * BS : 4 * WIDE + (sec + 1) * BS] = cross.astype(BF16)


def place_kernel(j_ref, r_ref, out_ref, acc):
    acc[...] = jnp.zeros_like(acc)

    def step(c, carry):
        for s in range(OUTSLOTS):
            at = j_ref[c, s]
            acc[at] += r_ref[c, :, s * BS : (s + 1) * BS].astype(F32)
        return carry

    lax.fori_loop(0, COLS, step, 0)
    for block in range(NCB):
        out_ref[:, block * BS : (block + 1) * BS] = acc[block]


VMEM = pl.BlockSpec(memory_space=pltpu.VMEM)
SMEM = pl.BlockSpec(memory_space=pltpu.SMEM)


def body(a_blocks, a_mask, p_blocks, p_mask, section_owner, agg_order):
    area = a_blocks.shape[2]
    row, col = lax.axis_index("row"), lax.axis_index("col")
    rows = row * BR + jnp.arange(BR, dtype=jnp.int32)

    band = band_columns(rows, agg_order)
    cross = ((rows // 16 + 4) % COLS) * BR + rows % BR
    live = jnp.stack([jnp.ones_like(rows)] * 3 + [1 - rows % 2], axis=-1) > 0
    fresh = ~jnp.any((band == cross[:, None]) & live, axis=1)
    wanted = jnp.concatenate([band, cross[:, None]], axis=1)
    usable = jnp.concatenate([live, fresh[:, None]], axis=1)
    local = wanted[:, :, None] == col * BR + jnp.arange(BR, dtype=jnp.int32)
    pick = local & usable[:, :, None] & (p_mask[:, None, :] != 0)
    compact = jnp.einsum(
        "iuj,ijf->iuf", pick.astype(BF16), p_blocks, preferred_element_type=F32
    ).astype(BF16)

    masked = a_blocks * a_mask[:, :, None].astype(BF16)
    tiles = masked.reshape(BR, 2, COLS, area).transpose(2, 0, 1, 3).reshape(COLS, 2 * BR, area)
    first = lax.all_to_all(jnp.concatenate([tiles, compact], axis=1), "col", 0, 0, tiled=True)

    mine = jnp.sum(first[:, 2 * BR :].astype(F32), axis=0).astype(BF16)
    mine = mine.reshape(USLOTS, BS, BS).transpose(1, 0, 2).reshape(BS, USLOTS * BS)
    mine = jnp.pad(mine, ((0, 0), (0, PW - USLOTS * BS)))
    p_rows = lax.all_to_all(
        jnp.broadcast_to(mine[None], (COLS, BS, PW)), "col", 0, 0, tiled=True
    )

    parts = [
        lax.dynamic_index_in_dim(first, section_owner[s], 0, keepdims=False)[: 2 * BR]
        for s in range(2)
    ]
    a_part = jnp.stack(parts).reshape(2, BR, 2, BS, BS).transpose(1, 3, 0, 2, 4).reshape(BR, BS, WIDE)

    spread, own = pl.pallas_call(
        partial_kernel,
        out_shape=(
            jax.ShapeDtypeStruct((ROWS, SLOTS, LANES), BF16),
            jax.ShapeDtypeStruct((4, BS, WIDE), F32),
        ),
        in_specs=[VMEM] * 3,
        out_specs=(VMEM, VMEM),
        scratch_shapes=[pltpu.VMEM((SLOTS, BS, WIDE), F32)],
        name="partial",
    )(p_rows, mine, a_part)
    spread = lax.all_to_all(spread, "row", 0, 0, tiled=True)

    every = jnp.arange(ROWS, dtype=jnp.int32)[:, None]
    slot = jnp.arange(SLOTS, dtype=jnp.int32)[None, :]
    target = jnp.where(
        slot == 0,
        (4 * every + NCB - 1) % NCB,
        jnp.where(slot == 1, (4 * every + 4) % NCB, (4 * every + slot - 2 + NCB // 2) % NCB),
    )
    source = jnp.where(slot < 6, lookup(agg_order, target), ((every // 2 + 4) % COLS) * BR + slot - 6)
    source = jnp.where(slot < 14, source, -1).reshape(-1)
    from_row = (jnp.broadcast_to(every, (ROWS, SLOTS)) * SLOTS + slot).reshape(-1)
    home = agg_order.reshape(ROWS, 4)
    near = jnp.concatenate([home, home, jnp.full((ROWS, 8), -2, jnp.int32)], axis=1).reshape(-1)
    tail = jnp.arange(8, dtype=jnp.int32)
    panel = (2 * lookup(section_owner, tail // 4) + (tail // 2) % 2) * SLOTS + 14 + tail % 2
    panel = jnp.concatenate([jnp.full((8,), -1, jnp.int32), panel])
    panel = jnp.broadcast_to(panel[None], (ROWS, SLOTS)).reshape(-1)
    choose = (near[:, None] == source[None]) | (panel[:, None] == from_row[None])
    total = jnp.dot(
        choose.astype(BF16), spread.reshape(ROWS * SLOTS, LANES), preferred_element_type=F32
    )
    high = total.astype(BF16)
    low = (total - high.astype(F32)).astype(BF16)
    is_low = (jnp.arange(ROWS * SLOTS) % SLOTS // 4 == 1)[:, None]
    back = jnp.where(is_low, low, high).reshape(ROWS, SLOTS, LANES)
    back = lax.all_to_all(back, "row", 0, 0, tiled=True)

    outs = pl.pallas_call(
        product_kernel,
        out_shape=jax.ShapeDtypeStruct((4 * BS, OUTSLOTS * BS), BF16),
        in_specs=[VMEM] * 2,
        out_specs=VMEM,
        scratch_shapes=[pltpu.VMEM((SLOTS, BS, WIDE), F32), pltpu.VMEM((4, BS, BS), F32)],
        name="product",
    )(back, own)
    outs = lax.all_to_all(outs.reshape(COLS, 4 * BS // COLS, OUTSLOTS * BS), "col", 0, 0, tiled=True)

    k_col = jnp.arange(COLS, dtype=jnp.int32)[:, None, None]
    k_sec = section_owner[None, :, None]
    k_half = jnp.arange(2, dtype=jnp.int32)[None, None, :]
    k_rows = 2 * BR * k_sec + BR * k_half + k_col
    j_band = band_columns(k_rows, agg_order).reshape(COLS, 4 * KK)
    j_cross = ((k_sec + 4) % COLS)[:, :, 0] * BR + k_col[:, :, 0]
    j_table = jnp.concatenate([j_band, j_cross], axis=1)
    return pl.pallas_call(
        place_kernel,
        out_shape=jax.ShapeDtypeStruct((4 * BS // COLS, NCB * BS), F32),
        in_specs=[SMEM, VMEM],
        out_specs=VMEM,
        scratch_shapes=[pltpu.VMEM((NCB, 4 * BS // COLS, BS), F32)],
        name="place",
    )(j_table, outs)


def solution(mesh):
    in_specs = (
        P("row", "col", None),
        P("row", "col"),
        P("row", "col", None),
        P("row", "col"),
        P(),
        P(),
    )
    out_specs = P(("row", "col"), None)
    return jax.shard_map(body, mesh=mesh, in_specs=in_specs, out_specs=out_specs, check_vma=False)
```

```python
import jax
import jax.numpy as jnp
from jax import lax
from jax.experimental import pallas as pl
from jax.experimental.pallas import tpu as pltpu
from jax.sharding import PartitionSpec as P

BS = 96
BR = 8
NCB = 64
KK = 4
WIDE = KK * BS
ROWS = 16
COLS = 8
PIECE = BS // ROWS
LANES = PIECE * WIDE
USLOTS = 5
PW = 512
OUTSLOTS = 18
F32 = jnp.float32
BF16 = jnp.bfloat16


def lookup(table, index):
    hit = index[..., None] == jnp.arange(table.shape[0], dtype=jnp.int32)
    return jnp.sum(jnp.where(hit, table, 0), axis=-1)


def shift(value, axis, by):
    size = lax.axis_size(axis)
    return lax.ppermute(value, axis, [(i, (i + by) % size) for i in range(size)])


def band_columns(rows, agg_order):
    center = rows // 2
    places = jnp.stack(
        [(center + NCB - 1) % NCB, center, (center + 1) % NCB, (center + NCB // 2) % NCB], axis=-1
    )
    return lookup(agg_order, places)


def partial_kernel(c_ref, *refs):
    p_refs, (a_ref, x_ref, own_ref, prev_ref, next_ref, far_ref, later_ref, p_ref, scr) = (
        refs[:COLS],
        refs[COLS:],
    )
    later_ref[...] = p_refs[0][...]
    for d in range(COLS):
        p_ref[lax.rem(c_ref[0] + COLS - d, COLS)] = p_refs[d][...]
    total = [None] * 6
    for i in range(BR):
        q = lax.dot_general(
            p_ref[i], a_ref[i], (((0,), (0,)), ((), ())), preferred_element_type=F32
        )
        local = i // 2
        for u in range(3):
            w = local + u
            value = q[u * BS : (u + 1) * BS]
            total[w] = value if total[w] is None else total[w] + value
            last = min(local, w) == min(3, w) and i % 2 == 1
            if last and w == 0:
                prev_ref[...] = total[w].astype(BF16)
            elif last and w == 5:
                next_ref[...] = total[w].astype(BF16)
            elif last:
                own_ref[w - 1] = total[w]
        if i % 2 == 0:
            far_ref[local] = q[3 * BS : 4 * BS].astype(BF16)
        scr[i] = q[4 * BS : 5 * BS]
    for octet in range(BS // 8):
        chunk = jnp.swapaxes(scr[:, octet * 8 : octet * 8 + 8, :], 0, 1)
        for e in range(8):
            j, pp = divmod(octet * 8 + e, PIECE)
            x_ref[j, :, pp * WIDE : (pp + 1) * WIDE] = chunk[e].astype(BF16)


def product_kernel(c_ref, r_ref, own_ref, prev_ref, next_ref, far_ref, p_ref, o_ref, x_ref, scr, held):
    for octet in range(BS // 8):
        rows = []
        for e in range(8):
            j, pp = divmod(octet * 8 + e, PIECE)
            rows.append(r_ref[j, :, pp * WIDE : (pp + 1) * WIDE].astype(F32))
        scr[:, octet * 8 : octet * 8 + 8, :] = jnp.swapaxes(jnp.stack(rows), 0, 1)
    for t in range(4):
        g = own_ref[t] + far_ref[t].astype(F32)
        if t == 0:
            g = g + prev_ref[...].astype(F32)
        if t == 3:
            g = g + next_ref[...].astype(F32)
        scr[t] = g + (scr[t] + scr[4 + t])
    for kk in range(KK):
        here = c_ref[0] == kk % 2
        right = jnp.where(here, p_ref[kk // 2], o_ref[kk // 2])[:, : USLOTS * BS]
        for t in range(4):
            g = scr[t, :, kk * BS : (kk + 1) * BS]
            high = g.astype(BF16)
            low = (g - high.astype(F32)).astype(BF16)
            out = jnp.dot(high, right, preferred_element_type=F32)
            out = out + jnp.dot(low, right, preferred_element_type=F32)
            span = slice(t * BS, (t + 1) * BS)
            x_ref[span, kk * WIDE : (kk + 1) * WIDE] = out[:, :WIDE].astype(BF16)
            if kk % 2 == 0:
                held[t] = out[:, WIDE:]
            else:
                sec = kk // 2
                cross = held[t] + out[:, WIDE:]
                x_ref[span, 4 * WIDE + sec * BS : 4 * WIDE + (sec + 1) * BS] = cross.astype(BF16)


def place_kernel(j_ref, r_ref, out_ref, acc):
    acc[...] = jnp.zeros_like(acc)

    def step(c, carry):
        for s in range(OUTSLOTS):
            at = j_ref[c, s]
            acc[at] += r_ref[c, :, s * BS : (s + 1) * BS].astype(F32)
        return carry

    lax.fori_loop(0, COLS, step, 0)
    for block in range(NCB):
        out_ref[:, block * BS : (block + 1) * BS] = acc[block]


VMEM = pl.BlockSpec(memory_space=pltpu.VMEM)
SMEM = pl.BlockSpec(memory_space=pltpu.SMEM)


def body(a_blocks, a_mask, p_blocks, p_mask, section_owner, agg_order):
    area = a_blocks.shape[2]
    row, col = lax.axis_index("row"), lax.axis_index("col")
    rows = row * BR + jnp.arange(BR, dtype=jnp.int32)

    band = band_columns(rows, agg_order)
    cross = ((rows // 16 + 4) % COLS) * BR + rows % BR
    live = jnp.stack([jnp.ones_like(rows)] * 3 + [1 - rows % 2], axis=-1) > 0
    fresh = ~jnp.any((band == cross[:, None]) & live, axis=1)
    wanted = jnp.concatenate([band, cross[:, None]], axis=1)
    usable = jnp.concatenate([live, fresh[:, None]], axis=1)
    local = wanted[:, :, None] == col * BR + jnp.arange(BR, dtype=jnp.int32)
    pick = local & usable[:, :, None] & (p_mask[:, None, :] != 0)
    compact = jnp.einsum(
        "iuj,ijf->iuf", pick.astype(BF16), p_blocks, preferred_element_type=F32
    ).astype(BF16)

    masked = a_blocks * a_mask[:, :, None].astype(BF16)
    tiles = masked.reshape(BR, 2, COLS, area).transpose(2, 0, 1, 3).reshape(COLS, 2 * BR, area)
    tiles = lax.all_to_all(tiles, "col", 0, 0, tiled=True)
    mine = lax.dynamic_index_in_dim(compact, col, 0, keepdims=False).astype(F32)
    for d in range(1, COLS):
        piece = lax.dynamic_index_in_dim(compact, (col + d) % COLS, 0, keepdims=False)
        mine = mine + shift(piece, "col", d).astype(F32)
    mine = mine.astype(BF16)
    mine = mine.reshape(USLOTS, BS, BS).transpose(1, 0, 2).reshape(BS, USLOTS * BS)
    mine = jnp.pad(mine, ((0, 0), (0, PW - USLOTS * BS)))
    p_rows = [mine] + [shift(mine, "col", d) for d in range(1, COLS)]

    parts = [
        lax.dynamic_index_in_dim(tiles, section_owner[s], 0, keepdims=False) for s in range(2)
    ]
    a_part = jnp.stack(parts).reshape(2, BR, 2, BS, BS).transpose(1, 3, 0, 2, 4).reshape(BR, BS, WIDE)

    spread, own, prev_part, next_part, far_part, later = pl.pallas_call(
        partial_kernel,
        out_shape=(
            jax.ShapeDtypeStruct((ROWS, BR, LANES), BF16),
            jax.ShapeDtypeStruct((4, BS, WIDE), F32),
            jax.ShapeDtypeStruct((BS, WIDE), BF16),
            jax.ShapeDtypeStruct((BS, WIDE), BF16),
            jax.ShapeDtypeStruct((4, BS, WIDE), BF16),
            jax.ShapeDtypeStruct((BS, PW), BF16),
        ),
        in_specs=[SMEM] + [VMEM] * (COLS + 1),
        out_specs=(VMEM,) * 6,
        scratch_shapes=[pltpu.VMEM((COLS, BS, PW), BF16), pltpu.VMEM((BR, BS, WIDE), F32)],
        name="partial",
    )(col[None], *p_rows, a_part)
    spread = lax.all_to_all(spread, "row", 0, 0, tiled=True)
    from_next = shift(prev_part, "row", -1)
    from_prev = shift(next_part, "row", 1)
    from_far = shift(far_part, "row", ROWS // 2)
    p_cols = [later] + [shift(later, "row", 2 * e) for e in range(1, COLS)]
    chosen = []
    for s in range(2):
        away = (row // 2 - section_owner[s]) % COLS
        kept = p_cols[0]
        for e in range(1, COLS):
            kept = jnp.where(away == e, p_cols[e], kept)
        chosen.append(kept)
    chosen = jnp.stack(chosen)
    swapped = lax.ppermute(chosen, "row", [(r, r ^ 1) for r in range(ROWS)])

    row_id = jnp.arange(ROWS, dtype=jnp.int32)[:, None]
    source = ((row_id // 2 + 4) % COLS) * BR + jnp.arange(BR, dtype=jnp.int32)[None]
    home = agg_order.reshape(ROWS, 4)
    near = jnp.concatenate([home, home], axis=1)
    choose = near.reshape(-1)[:, None] == source.reshape(-1)[None]
    total = jnp.dot(
        choose.astype(BF16), spread.reshape(ROWS * BR, LANES), preferred_element_type=F32
    )
    high = lax.reduce_precision(total, 8, 7)
    is_low = (jnp.arange(ROWS * BR) % BR // 4 == 1)[:, None]
    back = jnp.where(is_low, total - high, high).astype(BF16).reshape(ROWS, BR, LANES)
    back = lax.all_to_all(back, "row", 0, 0, tiled=True)

    outs = pl.pallas_call(
        product_kernel,
        out_shape=jax.ShapeDtypeStruct((4 * BS, OUTSLOTS * BS), BF16),
        in_specs=[SMEM] + [VMEM] * 7,
        out_specs=VMEM,
        scratch_shapes=[pltpu.VMEM((BR, BS, WIDE), F32), pltpu.VMEM((4, BS, BS), F32)],
        name="product",
    )((row % 2)[None], back, own, from_prev, from_next, from_far, chosen, swapped)
    outs = lax.all_to_all(outs.reshape(COLS, 4 * BS // COLS, OUTSLOTS * BS), "col", 0, 0, tiled=True)

    k_col = jnp.arange(COLS, dtype=jnp.int32)[:, None, None]
    k_sec = section_owner[None, :, None]
    k_half = jnp.arange(2, dtype=jnp.int32)[None, None, :]
    k_rows = 2 * BR * k_sec + BR * k_half + k_col
    j_band = band_columns(k_rows, agg_order).reshape(COLS, 4 * KK)
    j_cross = ((k_sec + 4) % COLS)[:, :, 0] * BR + k_col[:, :, 0]
    j_table = jnp.concatenate([j_band, j_cross], axis=1)
    return pl.pallas_call(
        place_kernel,
        out_shape=jax.ShapeDtypeStruct((4 * BS // COLS, NCB * BS), F32),
        in_specs=[SMEM, VMEM],
        out_specs=VMEM,
        scratch_shapes=[pltpu.VMEM((NCB, 4 * BS // COLS, BS), F32)],
        name="place",
    )(j_table, outs)


def solution(mesh):
    in_specs = (
        P("row", "col", None),
        P("row", "col"),
        P("row", "col", None),
        P("row", "col"),
        P(),
        P(),
    )
    out_specs = P(("row", "col"), None)
    return jax.shard_map(body, mesh=mesh, in_specs=in_specs, out_specs=out_specs, check_vma=False)
```

```python
import jax
import jax.numpy as jnp
from jax import lax
from jax.experimental import pallas as pl
from jax.experimental.pallas import tpu as pltpu
from jax.sharding import PartitionSpec as P

BS = 96
BR = 8
NCB = 64
KK = 4
WIDE = KK * BS
ROWS = 16
COLS = 8
PIECE = BS // ROWS
LANES = PIECE * WIDE
USLOTS = 5
PW = 512
OUTSLOTS = 18
F32 = jnp.float32
BF16 = jnp.bfloat16


def lookup(table, index):
    hit = index[..., None] == jnp.arange(table.shape[0], dtype=jnp.int32)
    return jnp.sum(jnp.where(hit, table, 0), axis=-1)


def shift(value, axis, by):
    size = lax.axis_size(axis)
    return lax.ppermute(value, axis, [(i, (i + by) % size) for i in range(size)])


def band_columns(rows, agg_order):
    center = rows // 2
    places = jnp.stack(
        [(center + NCB - 1) % NCB, center, (center + 1) % NCB, (center + NCB // 2) % NCB], axis=-1
    )
    return lookup(agg_order, places)


def partial_kernel(c_ref, *refs):
    p_refs, (a_ref, x_ref, own_ref, prev_ref, next_ref, far_ref, later_ref, p_ref, scr) = (
        refs[:COLS],
        refs[COLS:],
    )
    later_ref[...] = p_refs[0][...]
    for d in range(COLS):
        p_ref[lax.rem(c_ref[0] + COLS - d, COLS)] = p_refs[d][...]
    total = [None] * 6
    for i in range(BR):
        q = lax.dot_general(
            p_ref[i], a_ref[i], (((0,), (0,)), ((), ())), preferred_element_type=F32
        )
        local = i // 2
        for u in range(3):
            w = local + u
            value = q[u * BS : (u + 1) * BS]
            total[w] = value if total[w] is None else total[w] + value
            last = min(local, w) == min(3, w) and i % 2 == 1
            if last and w == 0:
                prev_ref[...] = total[w].astype(BF16)
            elif last and w == 5:
                next_ref[...] = total[w].astype(BF16)
            elif last:
                own_ref[w - 1] = total[w]
        if i % 2 == 0:
            far_ref[local] = q[3 * BS : 4 * BS].astype(BF16)
        scr[i] = q[4 * BS : 5 * BS]
    for octet in range(BS // 8):
        chunk = jnp.swapaxes(scr[:, octet * 8 : octet * 8 + 8, :], 0, 1)
        for e in range(8):
            j, pp = divmod(octet * 8 + e, PIECE)
            x_ref[j, :, pp * WIDE : (pp + 1) * WIDE] = chunk[e].astype(BF16)


def product_kernel(c_ref, r_ref, own_ref, prev_ref, next_ref, far_ref, p_ref, o_ref, x_ref, scr, held):
    for octet in range(BS // 8):
        rows = []
        for e in range(8):
            j, pp = divmod(octet * 8 + e, PIECE)
            rows.append(r_ref[j, :, pp * WIDE : (pp + 1) * WIDE].astype(F32))
        scr[:, octet * 8 : octet * 8 + 8, :] = jnp.swapaxes(jnp.stack(rows), 0, 1)
    for t in range(4):
        g = own_ref[t] + far_ref[t].astype(F32)
        if t == 0:
            g = g + prev_ref[...].astype(F32)
        if t == 3:
            g = g + next_ref[...].astype(F32)
        scr[t] = g + (scr[t] + scr[4 + t])
    for kk in range(KK):
        here = c_ref[0] == kk % 2
        right = jnp.where(here, p_ref[kk // 2], o_ref[kk // 2])[:, : USLOTS * BS]
        for t in range(4):
            g = scr[t, :, kk * BS : (kk + 1) * BS]
            high = g.astype(BF16)
            low = (g - high.astype(F32)).astype(BF16)
            out = jnp.dot(high, right, preferred_element_type=F32)
            out = out + jnp.dot(low, right, preferred_element_type=F32)
            span = slice(t * BS, (t + 1) * BS)
            x_ref[span, kk * WIDE : (kk + 1) * WIDE] = out[:, :WIDE].astype(BF16)
            if kk % 2 == 0:
                held[t] = out[:, WIDE:]
            else:
                sec = kk // 2
                cross = held[t] + out[:, WIDE:]
                x_ref[span, 4 * WIDE + sec * BS : 4 * WIDE + (sec + 1) * BS] = cross.astype(BF16)


def place_kernel(j_ref, r_ref, out_ref, acc):
    acc[...] = jnp.zeros_like(acc)

    def step(c, carry):
        for s in range(OUTSLOTS):
            at = j_ref[c, s]
            acc[at] += r_ref[c, :, s * BS : (s + 1) * BS].astype(F32)
        return carry

    lax.fori_loop(0, COLS, step, 0)
    for block in range(NCB):
        out_ref[:, block * BS : (block + 1) * BS] = acc[block]


VMEM = pl.BlockSpec(memory_space=pltpu.VMEM)
SMEM = pl.BlockSpec(memory_space=pltpu.SMEM)


def body(a_blocks, a_mask, p_blocks, p_mask, section_owner, agg_order):
    area = a_blocks.shape[2]
    row, col = lax.axis_index("row"), lax.axis_index("col")
    rows = row * BR + jnp.arange(BR, dtype=jnp.int32)

    band = band_columns(rows, agg_order)
    cross = ((rows // 16 + 4) % COLS) * BR + rows % BR
    live = jnp.stack([jnp.ones_like(rows)] * 3 + [1 - rows % 2], axis=-1) > 0
    fresh = ~jnp.any((band == cross[:, None]) & live, axis=1)
    wanted = jnp.concatenate([band, cross[:, None]], axis=1)
    usable = jnp.concatenate([live, fresh[:, None]], axis=1)
    masked = a_blocks * a_mask[:, :, None].astype(BF16)
    tiles = masked.reshape(BR, 2, COLS, area).transpose(2, 0, 1, 3).reshape(COLS, 2 * BR, area)
    tiles, p_blocks = lax.optimization_barrier((tiles, p_blocks))
    tiles = lax.all_to_all(tiles, "col", 0, 0, tiled=True)
    local = wanted[:, :, None] == col * BR + jnp.arange(BR, dtype=jnp.int32)
    pick = local & usable[:, :, None] & (p_mask[:, None, :] != 0)
    compact = jnp.einsum(
        "iuj,ijf->iuf", pick.astype(BF16), p_blocks, preferred_element_type=F32
    ).astype(BF16)

    mine = lax.dynamic_index_in_dim(compact, col, 0, keepdims=False).astype(F32)
    for d in range(1, COLS):
        piece = lax.dynamic_index_in_dim(compact, (col + d) % COLS, 0, keepdims=False)
        mine = mine + shift(piece, "col", d).astype(F32)
    mine = mine.astype(BF16)
    mine = mine.reshape(USLOTS, BS, BS).transpose(1, 0, 2).reshape(BS, USLOTS * BS)
    mine = jnp.pad(mine, ((0, 0), (0, PW - USLOTS * BS)))
    p_rows = [mine] + [shift(mine, "col", d) for d in range(1, COLS)]

    parts = [
        lax.dynamic_index_in_dim(tiles, section_owner[s], 0, keepdims=False) for s in range(2)
    ]
    a_part = jnp.stack(parts).reshape(2, BR, 2, BS, BS).transpose(1, 3, 0, 2, 4).reshape(BR, BS, WIDE)

    spread, own, prev_part, next_part, far_part, later = pl.pallas_call(
        partial_kernel,
        out_shape=(
            jax.ShapeDtypeStruct((ROWS, BR, LANES), BF16),
            jax.ShapeDtypeStruct((4, BS, WIDE), F32),
            jax.ShapeDtypeStruct((BS, WIDE), BF16),
            jax.ShapeDtypeStruct((BS, WIDE), BF16),
            jax.ShapeDtypeStruct((4, BS, WIDE), BF16),
            jax.ShapeDtypeStruct((BS, PW), BF16),
        ),
        in_specs=[SMEM] + [VMEM] * (COLS + 1),
        out_specs=(VMEM,) * 6,
        scratch_shapes=[pltpu.VMEM((COLS, BS, PW), BF16), pltpu.VMEM((BR, BS, WIDE), F32)],
        name="partial",
    )(col[None], *p_rows, a_part)
    spread = lax.all_to_all(spread, "row", 0, 0, tiled=True)
    from_next = shift(prev_part, "row", -1)
    from_prev = shift(next_part, "row", 1)
    from_far = shift(far_part, "row", ROWS // 2)
    chosen = jnp.stack([later, later])
    for bit in range(3):
        moved = lax.ppermute(chosen, "row", [(r, r ^ (2 << bit)) for r in range(ROWS)])
        wrong = (((row // 2) ^ section_owner) >> bit) & 1
        chosen = jnp.where(wrong[:, None, None] == 1, moved, chosen)
    swapped = lax.ppermute(chosen, "row", [(r, r ^ 1) for r in range(ROWS)])

    row_id = jnp.arange(ROWS, dtype=jnp.int32)[:, None]
    source = ((row_id // 2 + 4) % COLS) * BR + jnp.arange(BR, dtype=jnp.int32)[None]
    home = agg_order.reshape(ROWS, 4)
    near = jnp.concatenate([home, home], axis=1)
    choose = near.reshape(-1)[:, None] == source.reshape(-1)[None]
    total = jnp.dot(
        choose.astype(BF16), spread.reshape(ROWS * BR, LANES), preferred_element_type=F32
    )
    high = lax.reduce_precision(total, 8, 7)
    is_low = (jnp.arange(ROWS * BR) % BR // 4 == 1)[:, None]
    back = jnp.where(is_low, total - high, high).astype(BF16).reshape(ROWS, BR, LANES)
    back = lax.all_to_all(back, "row", 0, 0, tiled=True)

    outs = pl.pallas_call(
        product_kernel,
        out_shape=jax.ShapeDtypeStruct((4 * BS, OUTSLOTS * BS), BF16),
        in_specs=[SMEM] + [VMEM] * 7,
        out_specs=VMEM,
        scratch_shapes=[pltpu.VMEM((BR, BS, WIDE), F32), pltpu.VMEM((4, BS, BS), F32)],
        name="product",
    )((row % 2)[None], back, own, from_prev, from_next, from_far, chosen, swapped)
    outs = lax.all_to_all(outs.reshape(COLS, 4 * BS // COLS, OUTSLOTS * BS), "col", 0, 0, tiled=True)

    k_col = jnp.arange(COLS, dtype=jnp.int32)[:, None, None]
    k_sec = section_owner[None, :, None]
    k_half = jnp.arange(2, dtype=jnp.int32)[None, None, :]
    k_rows = 2 * BR * k_sec + BR * k_half + k_col
    j_band = band_columns(k_rows, agg_order).reshape(COLS, 4 * KK)
    j_cross = ((k_sec + 4) % COLS)[:, :, 0] * BR + k_col[:, :, 0]
    j_table = jnp.concatenate([j_band, j_cross], axis=1)
    return pl.pallas_call(
        place_kernel,
        out_shape=jax.ShapeDtypeStruct((4 * BS // COLS, NCB * BS), F32),
        in_specs=[SMEM, VMEM],
        out_specs=VMEM,
        scratch_shapes=[pltpu.VMEM((NCB, 4 * BS // COLS, BS), F32)],
        name="place",
    )(j_table, outs)


def solution(mesh):
    in_specs = (
        P("row", "col", None),
        P("row", "col"),
        P("row", "col", None),
        P("row", "col"),
        P(),
        P(),
    )
    out_specs = P(("row", "col"), None)
    return jax.shard_map(body, mesh=mesh, in_specs=in_specs, out_specs=out_specs, check_vma=False)
```

```python
import jax
import jax.numpy as jnp
from jax import lax
from jax.experimental import pallas as pl
from jax.experimental.pallas import tpu as pltpu
from jax.sharding import PartitionSpec as P

BS = 96
BR = 8
NCB = 64
KK = 4
WIDE = KK * BS
ROWS = 16
COLS = 8
PIECE = BS // ROWS
LANES = PIECE * WIDE
USLOTS = 5
PW = 512
OUTSLOTS = 18
F32 = jnp.float32
BF16 = jnp.bfloat16


def lookup(table, index):
    hit = index[..., None] == jnp.arange(table.shape[0], dtype=jnp.int32)
    return jnp.sum(jnp.where(hit, table, 0), axis=-1)


def shift(value, axis, by):
    size = lax.axis_size(axis)
    return lax.ppermute(value, axis, [(i, (i + by) % size) for i in range(size)])


def band_columns(rows, agg_order):
    center = rows // 2
    places = jnp.stack(
        [(center + NCB - 1) % NCB, center, (center + 1) % NCB, (center + NCB // 2) % NCB], axis=-1
    )
    return lookup(agg_order, places)


def partial_kernel(p_ref, a_ref, x_ref, own_ref, prev_ref, next_ref, far_ref, scr):
    total = [None] * 6
    for i in range(BR):
        q = lax.dot_general(
            p_ref[i], a_ref[i], (((0,), (0,)), ((), ())), preferred_element_type=F32
        )
        local = i // 2
        for u in range(3):
            w = local + u
            value = q[u * BS : (u + 1) * BS]
            total[w] = value if total[w] is None else total[w] + value
            last = min(local, w) == min(3, w) and i % 2 == 1
            if last and w == 0:
                prev_ref[...] = total[w].astype(BF16)
            elif last and w == 5:
                next_ref[...] = total[w].astype(BF16)
            elif last:
                own_ref[w - 1] = total[w]
        if i % 2 == 0:
            far_ref[local] = q[3 * BS : 4 * BS].astype(BF16)
        scr[i] = q[4 * BS : 5 * BS]
    for octet in range(BS // 8):
        chunk = jnp.swapaxes(scr[:, octet * 8 : octet * 8 + 8, :], 0, 1)
        for e in range(8):
            j, pp = divmod(octet * 8 + e, PIECE)
            x_ref[j, :, pp * WIDE : (pp + 1) * WIDE] = chunk[e].astype(BF16)


def product_kernel(c_ref, r_ref, own_ref, prev_ref, next_ref, far_ref, p_ref, o_ref, x_ref, scr, held):
    for octet in range(BS // 8):
        rows = []
        for e in range(8):
            j, pp = divmod(octet * 8 + e, PIECE)
            rows.append(r_ref[j, :, pp * WIDE : (pp + 1) * WIDE].astype(F32))
        scr[:, octet * 8 : octet * 8 + 8, :] = jnp.swapaxes(jnp.stack(rows), 0, 1)
    for t in range(4):
        g = own_ref[t] + far_ref[t].astype(F32)
        if t == 0:
            g = g + prev_ref[...].astype(F32)
        if t == 3:
            g = g + next_ref[...].astype(F32)
        scr[t] = g + (scr[t] + scr[4 + t])
    for kk in range(KK):
        here = c_ref[0] == kk % 2
        right = jnp.where(here, p_ref[kk // 2], o_ref[kk // 2])[:, : USLOTS * BS]
        for t in range(4):
            g = scr[t, :, kk * BS : (kk + 1) * BS]
            high = g.astype(BF16)
            low = (g - high.astype(F32)).astype(BF16)
            out = jnp.dot(high, right, preferred_element_type=F32)
            out = out + jnp.dot(low, right, preferred_element_type=F32)
            span = slice(t * BS, (t + 1) * BS)
            x_ref[span, kk * WIDE : (kk + 1) * WIDE] = out[:, :WIDE].astype(BF16)
            if kk % 2 == 0:
                held[t] = out[:, WIDE:]
            else:
                sec = kk // 2
                cross = held[t] + out[:, WIDE:]
                x_ref[span, 4 * WIDE + sec * BS : 4 * WIDE + (sec + 1) * BS] = cross.astype(BF16)


def place_kernel(j_ref, r_ref, out_ref, acc):
    acc[...] = jnp.zeros_like(acc)

    def step(c, carry):
        for s in range(OUTSLOTS):
            at = j_ref[c, s]
            acc[at] += r_ref[c, :, s * BS : (s + 1) * BS].astype(F32)
        return carry

    lax.fori_loop(0, COLS, step, 0)
    for block in range(NCB):
        out_ref[:, block * BS : (block + 1) * BS] = acc[block]


VMEM = pl.BlockSpec(memory_space=pltpu.VMEM)
SMEM = pl.BlockSpec(memory_space=pltpu.SMEM)


def inner(a_blocks, a_mask, p_blocks, p_mask, section_owner, agg_order):
    area = a_blocks.shape[2]
    row, col = lax.axis_index("row"), lax.axis_index("col")
    rows = row * BR + jnp.arange(BR, dtype=jnp.int32)

    band = band_columns(rows, agg_order)
    cross = ((rows // 16 + 4) % COLS) * BR + rows % BR
    live = jnp.stack([jnp.ones_like(rows)] * 3 + [1 - rows % 2], axis=-1) > 0
    fresh = ~jnp.any((band == cross[:, None]) & live, axis=1)
    wanted = jnp.concatenate([band, cross[:, None]], axis=1)
    usable = jnp.concatenate([live, fresh[:, None]], axis=1)
    local = wanted[:, :, None] == col * BR + jnp.arange(BR, dtype=jnp.int32)
    pick = local & usable[:, :, None] & (p_mask[:, None, :] != 0)
    compact = jnp.einsum(
        "iuj,ijf->iuf", pick.astype(BF16), p_blocks, preferred_element_type=F32
    ).astype(BF16)

    sent = lax.all_to_all(
        compact.reshape(COLS, USLOTS * area // 128, 128), "col", 0, 0, tiled=True
    )
    tiles = (a_blocks * a_mask[:, :, None].astype(BF16)).reshape(BR, 2, COLS, area)
    got = []
    for d in range(COLS):
        piece = lax.dynamic_index_in_dim(tiles, (col + d) % COLS, 2, keepdims=False)
        piece = piece.reshape(2 * BR, area)
        got.append(shift(piece, "col", d) if d else piece)
    mine = jnp.sum(sent.astype(F32), axis=0).astype(BF16)
    mine = mine.reshape(USLOTS, BS, BS).transpose(1, 0, 2).reshape(BS, USLOTS * BS)
    mine = jnp.pad(mine, ((0, 0), (0, PW - USLOTS * BS)))
    p_rows = lax.all_to_all(jnp.broadcast_to(mine[None], (COLS, BS, PW)), "col", 0, 0, tiled=True)
    chosen = jnp.stack([mine, mine])
    for bit in range(3):
        moved = lax.ppermute(chosen, "row", [(r, r ^ (2 << bit)) for r in range(ROWS)])
        wrong = (((row // 2) ^ section_owner) >> bit) & 1
        chosen = jnp.where(wrong[:, None, None] == 1, moved, chosen)
    swapped = lax.ppermute(chosen, "row", [(r, r ^ 1) for r in range(ROWS)])

    parts = []
    for s in range(2):
        away = (col - section_owner[s]) % COLS
        kept = got[0]
        for d in range(1, COLS):
            kept = jnp.where(away == d, got[d], kept)
        parts.append(kept)
    a_part = jnp.stack(parts).reshape(2, BR, 2, BS, BS).transpose(1, 3, 0, 2, 4).reshape(BR, BS, WIDE)

    spread, own, prev_part, next_part, far_part = pl.pallas_call(
        partial_kernel,
        out_shape=(
            jax.ShapeDtypeStruct((ROWS, BR, LANES), BF16),
            jax.ShapeDtypeStruct((4, BS, WIDE), F32),
            jax.ShapeDtypeStruct((BS, WIDE), BF16),
            jax.ShapeDtypeStruct((BS, WIDE), BF16),
            jax.ShapeDtypeStruct((4, BS, WIDE), BF16),
        ),
        in_specs=[VMEM] * 2,
        out_specs=(VMEM,) * 5,
        scratch_shapes=[pltpu.VMEM((BR, BS, WIDE), F32)],
        name="partial",
    )(p_rows, a_part)
    spread = lax.all_to_all(spread, "row", 0, 0, tiled=True)
    from_next = shift(prev_part, "row", -1)
    from_prev = shift(next_part, "row", 1)
    from_far = shift(far_part, "row", ROWS // 2)

    row_id = jnp.arange(ROWS, dtype=jnp.int32)[:, None]
    source = ((row_id // 2 + 4) % COLS) * BR + jnp.arange(BR, dtype=jnp.int32)[None]
    home = agg_order.reshape(ROWS, 4)
    near = jnp.concatenate([home, home], axis=1)
    choose = near.reshape(-1)[:, None] == source.reshape(-1)[None]
    total = jnp.dot(
        choose.astype(BF16), spread.reshape(ROWS * BR, LANES), preferred_element_type=F32
    )
    high = lax.reduce_precision(total, 8, 7)
    is_low = (jnp.arange(ROWS * BR) % BR // 4 == 1)[:, None]
    back = jnp.where(is_low, total - high, high).astype(BF16).reshape(ROWS, BR, LANES)
    back = lax.all_to_all(back, "row", 0, 0, tiled=True)

    outs = pl.pallas_call(
        product_kernel,
        out_shape=jax.ShapeDtypeStruct((4 * BS, OUTSLOTS * BS), BF16),
        in_specs=[SMEM] + [VMEM] * 7,
        out_specs=VMEM,
        scratch_shapes=[pltpu.VMEM((BR, BS, WIDE), F32), pltpu.VMEM((4, BS, BS), F32)],
        name="product",
    )((row % 2)[None], back, own, from_prev, from_next, from_far, chosen, swapped)
    outs = lax.all_to_all(outs.reshape(COLS, 4 * BS // COLS, OUTSLOTS * BS), "col", 0, 0, tiled=True)

    k_col = jnp.arange(COLS, dtype=jnp.int32)[:, None, None]
    k_sec = section_owner[None, :, None]
    k_half = jnp.arange(2, dtype=jnp.int32)[None, None, :]
    k_rows = 2 * BR * k_sec + BR * k_half + k_col
    j_band = band_columns(k_rows, agg_order).reshape(COLS, 4 * KK)
    j_cross = ((k_sec + 4) % COLS)[:, :, 0] * BR + k_col[:, :, 0]
    j_table = jnp.concatenate([j_band, j_cross], axis=1)
    return pl.pallas_call(
        place_kernel,
        out_shape=jax.ShapeDtypeStruct((4 * BS // COLS, NCB * BS), F32),
        in_specs=[SMEM, VMEM],
        out_specs=VMEM,
        scratch_shapes=[pltpu.VMEM((NCB, 4 * BS // COLS, BS), F32)],
        name="place",
    )(j_table, outs)


def solution(mesh):
    in_specs = (
        P("row", "col", None),
        P("row", "col"),
        P("row", "col", None),
        P("row", "col"),
        P(),
        P(),
    )
    out_specs = P(("row", "col"), None)
    return jax.shard_map(inner, mesh=mesh, in_specs=in_specs, out_specs=out_specs, check_vma=False)
```

```python
import jax
import jax.numpy as jnp
from jax import lax
from jax.experimental import pallas as pl
from jax.experimental.pallas import tpu as pltpu
from jax.sharding import PartitionSpec as P

BS = 96
BR = 8
NCB = 64
KK = 4
WIDE = KK * BS
ROWS = 16
COLS = 8
PIECE = BS // ROWS
LANES = PIECE * WIDE
USLOTS = 5
PW = 512
OUTSLOTS = 18
F32 = jnp.float32
BF16 = jnp.bfloat16


def lookup(table, index):
    hit = index[..., None] == jnp.arange(table.shape[0], dtype=jnp.int32)
    return jnp.sum(jnp.where(hit, table, 0), axis=-1)


def shift(value, axis, by):
    size = lax.axis_size(axis)
    return lax.ppermute(value, axis, [(i, (i + by) % size) for i in range(size)])


def band_columns(rows, agg_order):
    center = rows // 2
    places = jnp.stack(
        [(center + NCB - 1) % NCB, center, (center + 1) % NCB, (center + NCB // 2) % NCB], axis=-1
    )
    return lookup(agg_order, places)


def partial_kernel(s_ref, p_ref, *refs):
    got = refs[:COLS]
    x_ref, own_ref, prev_ref, next_ref, far_ref, scr, buf, a_ref, sem = refs[COLS:]
    for sec in range(2):
        for d in range(COLS):

            @pl.when(s_ref[sec] == d)
            def _():
                pltpu.make_async_copy(got[d], buf.at[sec], sem.at[sec]).start()

    for sec in range(2):
        pltpu.make_async_copy(got[0], buf.at[sec], sem.at[sec]).wait()
    for octet in range(BS // 8):
        for sec in range(2):
            rows = []
            for e in range(8):
                at = (octet * 8 + e) * BS
                rows.append(buf[sec, :, at : at + BS].astype(F32))
            turned = jnp.swapaxes(jnp.stack(rows), 0, 1)
            for row in range(2 * BR):
                kk = 2 * sec + row % 2
                a_ref[row // 2, octet * 8 : octet * 8 + 8, kk * BS : (kk + 1) * BS] = turned[row]
    total = [None] * 6
    for i in range(BR):
        q = lax.dot_general(
            p_ref[i], a_ref[i].astype(BF16), (((0,), (0,)), ((), ())), preferred_element_type=F32
        )
        local = i // 2
        for u in range(3):
            w = local + u
            value = q[u * BS : (u + 1) * BS]
            total[w] = value if total[w] is None else total[w] + value
            last = min(local, w) == min(3, w) and i % 2 == 1
            if last and w == 0:
                prev_ref[...] = total[w].astype(BF16)
            elif last and w == 5:
                next_ref[...] = total[w].astype(BF16)
            elif last:
                own_ref[w - 1] = total[w]
        if i % 2 == 0:
            far_ref[local] = q[3 * BS : 4 * BS].astype(BF16)
        scr[i] = q[4 * BS : 5 * BS]
    for octet in range(BS // 8):
        chunk = jnp.swapaxes(scr[:, octet * 8 : octet * 8 + 8, :], 0, 1)
        for e in range(8):
            j, pp = divmod(octet * 8 + e, PIECE)
            x_ref[j, :, pp * WIDE : (pp + 1) * WIDE] = chunk[e].astype(BF16)


def product_kernel(c_ref, r_ref, own_ref, prev_ref, next_ref, far_ref, p_ref, o_ref, x_ref, scr, held):
    for octet in range(BS // 8):
        rows = []
        for e in range(8):
            j, pp = divmod(octet * 8 + e, PIECE)
            rows.append(r_ref[j, :, pp * WIDE : (pp + 1) * WIDE].astype(F32))
        scr[:, octet * 8 : octet * 8 + 8, :] = jnp.swapaxes(jnp.stack(rows), 0, 1)
    for t in range(4):
        g = own_ref[t] + far_ref[t].astype(F32)
        if t == 0:
            g = g + prev_ref[...].astype(F32)
        if t == 3:
            g = g + next_ref[...].astype(F32)
        scr[t] = g + (scr[t] + scr[4 + t])
    for kk in range(KK):
        here = c_ref[0] == kk % 2
        right = jnp.where(here, p_ref[kk // 2], o_ref[kk // 2])[:, : USLOTS * BS]
        for t in range(4):
            g = scr[t, :, kk * BS : (kk + 1) * BS]
            high = g.astype(BF16)
            low = (g - high.astype(F32)).astype(BF16)
            out = jnp.dot(high, right, preferred_element_type=F32)
            out = out + jnp.dot(low, right, preferred_element_type=F32)
            span = slice(t * BS, (t + 1) * BS)
            x_ref[span, kk * WIDE : (kk + 1) * WIDE] = out[:, :WIDE].astype(BF16)
            if kk % 2 == 0:
                held[t] = out[:, WIDE:]
            else:
                sec = kk // 2
                cross = held[t] + out[:, WIDE:]
                x_ref[span, 4 * WIDE + sec * BS : 4 * WIDE + (sec + 1) * BS] = cross.astype(BF16)


def place_kernel(j_ref, r_ref, out_ref, acc):
    acc[...] = jnp.zeros_like(acc)

    def step(c, carry):
        for s in range(OUTSLOTS):
            at = j_ref[c, s]
            acc[at] += r_ref[c, :, s * BS : (s + 1) * BS].astype(F32)
        return carry

    lax.fori_loop(0, COLS, step, 0)
    for block in range(NCB):
        out_ref[:, block * BS : (block + 1) * BS] = acc[block]


VMEM = pl.BlockSpec(memory_space=pltpu.VMEM)
SMEM = pl.BlockSpec(memory_space=pltpu.SMEM)


def inner(a_blocks, a_mask, p_blocks, p_mask, section_owner, agg_order):
    area = a_blocks.shape[2]
    row, col = lax.axis_index("row"), lax.axis_index("col")
    rows = row * BR + jnp.arange(BR, dtype=jnp.int32)

    band = band_columns(rows, agg_order)
    cross = ((rows // 16 + 4) % COLS) * BR + rows % BR
    live = jnp.stack([jnp.ones_like(rows)] * 3 + [1 - rows % 2], axis=-1) > 0
    fresh = ~jnp.any((band == cross[:, None]) & live, axis=1)
    wanted = jnp.concatenate([band, cross[:, None]], axis=1)
    usable = jnp.concatenate([live, fresh[:, None]], axis=1)
    local = wanted[:, :, None] == col * BR + jnp.arange(BR, dtype=jnp.int32)
    pick = local & usable[:, :, None] & (p_mask[:, None, :] != 0)
    compact = jnp.einsum(
        "iuj,ijf->iuf", pick.astype(BF16), p_blocks, preferred_element_type=F32
    ).astype(BF16)

    sent = lax.all_to_all(
        compact.reshape(COLS, USLOTS * area // 128, 128), "col", 0, 0, tiled=True
    )
    line = jnp.arange(COLS * 2 * BR, dtype=jnp.int32)
    want = (line // 2) % BR * 2 * COLS + line % 2 * COLS + (col + line // (2 * BR)) % COLS
    order = jnp.where(want[:, None] == line[None], a_mask.reshape(1, -1), 0)
    tiles = jnp.dot(
        order.astype(BF16), a_blocks.reshape(2 * BR * COLS, area), preferred_element_type=F32
    ).astype(BF16)
    got = []
    for d in range(COLS):
        piece = tiles[2 * BR * d : 2 * BR * (d + 1)]
        got.append(shift(piece, "col", d) if d else piece)
    mine = jnp.sum(sent.astype(F32), axis=0).astype(BF16)
    mine = mine.reshape(USLOTS, BS, BS).transpose(1, 0, 2).reshape(BS, USLOTS * BS)
    mine = jnp.pad(mine, ((0, 0), (0, PW - USLOTS * BS)))
    p_rows = lax.all_to_all(jnp.broadcast_to(mine[None], (COLS, BS, PW)), "col", 0, 0, tiled=True)
    chosen = jnp.stack([mine, mine])
    for bit in range(3):
        moved = lax.ppermute(chosen, "row", [(r, r ^ (2 << bit)) for r in range(ROWS)])
        wrong = (((row // 2) ^ section_owner) >> bit) & 1
        chosen = jnp.where(wrong[:, None, None] == 1, moved, chosen)
    swapped = lax.ppermute(chosen, "row", [(r, r ^ 1) for r in range(ROWS)])

    away = (col - section_owner) % COLS
    spread, own, prev_part, next_part, far_part = pl.pallas_call(
        partial_kernel,
        out_shape=(
            jax.ShapeDtypeStruct((ROWS, BR, LANES), BF16),
            jax.ShapeDtypeStruct((4, BS, WIDE), F32),
            jax.ShapeDtypeStruct((BS, WIDE), BF16),
            jax.ShapeDtypeStruct((BS, WIDE), BF16),
            jax.ShapeDtypeStruct((4, BS, WIDE), BF16),
        ),
        in_specs=[SMEM, VMEM] + [pl.BlockSpec(memory_space=pl.ANY)] * COLS,
        out_specs=(VMEM,) * 5,
        scratch_shapes=[
            pltpu.VMEM((BR, BS, WIDE), F32),
            pltpu.VMEM((2, 2 * BR, area), BF16),
            pltpu.VMEM((BR, BS, WIDE), F32),
            pltpu.SemaphoreType.DMA((2,)),
        ],
        name="partial",
    )(away, p_rows, *got)
    spread = lax.all_to_all(spread, "row", 0, 0, tiled=True)
    from_next = shift(prev_part, "row", -1)
    from_prev = shift(next_part, "row", 1)
    from_far = shift(far_part, "row", ROWS // 2)

    row_id = jnp.arange(ROWS, dtype=jnp.int32)[:, None]
    source = ((row_id // 2 + 4) % COLS) * BR + jnp.arange(BR, dtype=jnp.int32)[None]
    home = agg_order.reshape(ROWS, 4)
    near = jnp.concatenate([home, home], axis=1)
    choose = near.reshape(-1)[:, None] == source.reshape(-1)[None]
    total = jnp.dot(
        choose.astype(BF16), spread.reshape(ROWS * BR, LANES), preferred_element_type=F32
    )
    high = lax.reduce_precision(total, 8, 7)
    is_low = (jnp.arange(ROWS * BR) % BR // 4 == 1)[:, None]
    back = jnp.where(is_low, total - high, high).astype(BF16).reshape(ROWS, BR, LANES)
    back = lax.all_to_all(back, "row", 0, 0, tiled=True)

    outs = pl.pallas_call(
        product_kernel,
        out_shape=jax.ShapeDtypeStruct((4 * BS, OUTSLOTS * BS), BF16),
        in_specs=[SMEM] + [VMEM] * 7,
        out_specs=VMEM,
        scratch_shapes=[pltpu.VMEM((BR, BS, WIDE), F32), pltpu.VMEM((4, BS, BS), F32)],
        name="product",
    )((row % 2)[None], back, own, from_prev, from_next, from_far, chosen, swapped)
    outs = lax.all_to_all(outs.reshape(COLS, 4 * BS // COLS, OUTSLOTS * BS), "col", 0, 0, tiled=True)

    k_col = jnp.arange(COLS, dtype=jnp.int32)[:, None, None]
    k_sec = section_owner[None, :, None]
    k_half = jnp.arange(2, dtype=jnp.int32)[None, None, :]
    k_rows = 2 * BR * k_sec + BR * k_half + k_col
    j_band = band_columns(k_rows, agg_order).reshape(COLS, 4 * KK)
    j_cross = ((k_sec + 4) % COLS)[:, :, 0] * BR + k_col[:, :, 0]
    j_table = jnp.concatenate([j_band, j_cross], axis=1)
    return pl.pallas_call(
        place_kernel,
        out_shape=jax.ShapeDtypeStruct((4 * BS // COLS, NCB * BS), F32),
        in_specs=[SMEM, VMEM],
        out_specs=VMEM,
        scratch_shapes=[pltpu.VMEM((NCB, 4 * BS // COLS, BS), F32)],
        name="place",
    )(j_table, outs)


def solution(mesh):
    in_specs = (
        P("row", "col", None),
        P("row", "col"),
        P("row", "col", None),
        P("row", "col"),
        P(),
        P(),
    )
    out_specs = P(("row", "col"), None)
    return jax.shard_map(inner, mesh=mesh, in_specs=in_specs, out_specs=out_specs, check_vma=False)
```

```python
import jax
import jax.numpy as jnp
from jax import lax
from jax.experimental import pallas as pl
from jax.experimental.pallas import tpu as pltpu
from jax.sharding import PartitionSpec as P

BS = 96
BR = 8
NCB = 64
KK = 4
WIDE = KK * BS
ROWS = 16
COLS = 8
PIECE = BS // ROWS
LANES = PIECE * WIDE
USLOTS = 5
PW = 512
OUTSLOTS = 12
F32 = jnp.float32
BF16 = jnp.bfloat16


def lookup(table, index):
    hit = index[..., None] == jnp.arange(table.shape[0], dtype=jnp.int32)
    return jnp.sum(jnp.where(hit, table, 0), axis=-1)


def shift(value, axis, by):
    size = lax.axis_size(axis)
    return lax.ppermute(value, axis, [(i, (i + by) % size) for i in range(size)])


def band_columns(rows, agg_order):
    center = rows // 2
    places = jnp.stack(
        [(center + NCB - 1) % NCB, center, (center + 1) % NCB, (center + NCB // 2) % NCB], axis=-1
    )
    return lookup(agg_order, places)


def partial_kernel(s_ref, p_ref, *refs):
    got = refs[:COLS]
    x_ref, own_ref, prev_ref, next_ref, far_ref, scr, buf, a_ref, sem = refs[COLS:]
    for sec in range(2):
        for d in range(COLS):

            @pl.when(s_ref[sec] == d)
            def _():
                pltpu.make_async_copy(got[d], buf.at[sec], sem.at[sec]).start()

    for sec in range(2):
        pltpu.make_async_copy(got[0], buf.at[sec], sem.at[sec]).wait()
    for octet in range(BS // 8):
        for sec in range(2):
            rows = []
            for e in range(8):
                at = (octet * 8 + e) * BS
                rows.append(buf[sec, :, at : at + BS].astype(F32))
            turned = jnp.swapaxes(jnp.stack(rows), 0, 1)
            for row in range(2 * BR):
                kk = 2 * sec + row % 2
                a_ref[row // 2, octet * 8 : octet * 8 + 8, kk * BS : (kk + 1) * BS] = turned[row]
    total = [None] * 6
    for i in range(BR):
        q = lax.dot_general(
            p_ref[i], a_ref[i].astype(BF16), (((0,), (0,)), ((), ())), preferred_element_type=F32
        )
        local = i // 2
        for u in range(3):
            w = local + u
            value = q[u * BS : (u + 1) * BS]
            total[w] = value if total[w] is None else total[w] + value
            last = min(local, w) == min(3, w) and i % 2 == 1
            if last and w == 0:
                prev_ref[...] = total[w].astype(BF16)
            elif last and w == 5:
                next_ref[...] = total[w].astype(BF16)
            elif last:
                own_ref[w - 1] = total[w]
        if i % 2 == 0:
            far_ref[local] = q[3 * BS : 4 * BS].astype(BF16)
        scr[i] = q[4 * BS : 5 * BS]
    for octet in range(BS // 8):
        chunk = jnp.swapaxes(scr[:, octet * 8 : octet * 8 + 8, :], 0, 1)
        for e in range(8):
            j, pp = divmod(octet * 8 + e, PIECE)
            x_ref[j, :, pp * WIDE : (pp + 1) * WIDE] = chunk[e].astype(BF16)


def product_kernel(c_ref, r_ref, own_ref, prev_ref, next_ref, far_ref, p_ref, o_ref, x_ref, scr):
    for octet in range(BS // 8):
        rows = []
        for e in range(8):
            j, pp = divmod(octet * 8 + e, PIECE)
            rows.append(r_ref[j, :, pp * WIDE : (pp + 1) * WIDE].astype(F32))
        scr[:, octet * 8 : octet * 8 + 8, :] = jnp.swapaxes(jnp.stack(rows), 0, 1)
    for t in range(4):
        g = own_ref[t] + far_ref[t].astype(F32)
        if t == 0:
            g = g + prev_ref[...].astype(F32)
        if t == 3:
            g = g + next_ref[...].astype(F32)
        scr[t] = g + (scr[t] + scr[4 + t])
    for sec in range(2):
        rights = []
        for e in range(2):
            here = c_ref[0] == e
            rights.append(jnp.where(here, p_ref[sec], o_ref[sec])[:, : USLOTS * BS])
        for t in range(4):
            outs = []
            for e in range(2):
                kk = 2 * sec + e
                g = scr[t, :, kk * BS : (kk + 1) * BS]
                high = g.astype(BF16)
                low = (g - high.astype(F32)).astype(BF16)
                out = jnp.dot(high, rights[e], preferred_element_type=F32)
                outs.append(out + jnp.dot(low, rights[e], preferred_element_type=F32))
            span = slice(t * BS, (t + 1) * BS)
            base = sec * OUTSLOTS // 2 * BS
            band = outs[0][:, : 3 * BS] + outs[1][:, : 3 * BS]
            x_ref[span, base : base + 3 * BS] = band.astype(BF16)
            x_ref[span, base + 3 * BS : base + 5 * BS] = outs[0][:, 3 * BS :].astype(BF16)
            x_ref[span, base + 5 * BS : base + 6 * BS] = outs[1][:, 4 * BS :].astype(BF16)


def place_kernel(j_ref, r_ref, out_ref, acc):
    acc[...] = jnp.zeros_like(acc)

    def step(c, carry):
        for s in range(OUTSLOTS):
            at = j_ref[c, s]
            acc[at] += r_ref[c, :, s * BS : (s + 1) * BS].astype(F32)
        return carry

    lax.fori_loop(0, COLS, step, 0)
    for block in range(NCB):
        out_ref[:, block * BS : (block + 1) * BS] = acc[block]


VMEM = pl.BlockSpec(memory_space=pltpu.VMEM)
SMEM = pl.BlockSpec(memory_space=pltpu.SMEM)


def inner(a_blocks, a_mask, p_blocks, p_mask, section_owner, agg_order):
    area = a_blocks.shape[2]
    row, col = lax.axis_index("row"), lax.axis_index("col")
    rows = row * BR + jnp.arange(BR, dtype=jnp.int32)

    band = band_columns(rows, agg_order)
    cross = ((rows // 16 + 4) % COLS) * BR + rows % BR
    live = jnp.stack([jnp.ones_like(rows)] * 3 + [1 - rows % 2], axis=-1) > 0
    fresh = ~jnp.any((band == cross[:, None]) & live, axis=1)
    wanted = jnp.concatenate([band, cross[:, None]], axis=1)
    usable = jnp.concatenate([live, fresh[:, None]], axis=1)
    local = wanted[:, :, None] == col * BR + jnp.arange(BR, dtype=jnp.int32)
    pick = local & usable[:, :, None] & (p_mask[:, None, :] != 0)
    compact = jnp.einsum(
        "iuj,ijf->iuf", pick.astype(BF16), p_blocks, preferred_element_type=F32
    ).astype(BF16)

    sent = lax.all_to_all(compact.reshape(COLS, USLOTS * area // 128, 128), "col", 0, 0, tiled=True)
    line = jnp.arange(COLS * 2 * BR, dtype=jnp.int32)
    heir = (col + line // (2 * BR)) % COLS
    want = (line // 2) % BR * 2 * COLS + 2 * (heir // 2 + 4 * (heir % 2)) + line % 2
    order = jnp.where(want[:, None] == line[None], a_mask.reshape(1, -1), 0)
    tiles = jnp.dot(
        order.astype(BF16), a_blocks.reshape(2 * BR * COLS, area), preferred_element_type=F32
    ).astype(BF16)
    got = []
    for d in range(COLS):
        piece = tiles[2 * BR * d : 2 * BR * (d + 1)]
        got.append(shift(piece, "col", d) if d else piece)
    mine = jnp.sum(sent.astype(F32), axis=0).astype(BF16)
    mine = mine.reshape(USLOTS, BS, BS).transpose(1, 0, 2).reshape(BS, USLOTS * BS)
    mine = jnp.pad(mine, ((0, 0), (0, PW - USLOTS * BS)))
    p_rows = lax.all_to_all(jnp.broadcast_to(mine[None], (COLS, BS, PW)), "col", 0, 0, tiled=True)
    pairs = [
        (r * COLS + c, (r ^ 1) * COLS + (c ^ 1))
        for r in range(ROWS)
        for c in range(COLS)
        if r % 2 != c % 2
    ]
    other = lax.ppermute(mine, ("row", "col"), pairs)
    start = jnp.where(row % 2 == col % 2, mine, other)
    chosen = jnp.stack([start, start])
    for bit in range(3):
        moved = lax.ppermute(chosen, "row", [(r, r ^ (2 << bit)) for r in range(ROWS)])
        wrong = (((row // 2) ^ section_owner) >> bit) & 1
        chosen = jnp.where(wrong[:, None, None] == 1, moved, chosen)
    swapped = lax.ppermute(chosen, "row", [(r, r ^ 1) for r in range(ROWS)])

    away = (col - section_owner) % COLS
    spread, own, prev_part, next_part, far_part = pl.pallas_call(
        partial_kernel,
        out_shape=(
            jax.ShapeDtypeStruct((ROWS, BR, LANES), BF16),
            jax.ShapeDtypeStruct((4, BS, WIDE), F32),
            jax.ShapeDtypeStruct((BS, WIDE), BF16),
            jax.ShapeDtypeStruct((BS, WIDE), BF16),
            jax.ShapeDtypeStruct((4, BS, WIDE), BF16),
        ),
        in_specs=[SMEM, VMEM] + [pl.BlockSpec(memory_space=pl.ANY)] * COLS,
        out_specs=(VMEM,) * 5,
        scratch_shapes=[
            pltpu.VMEM((BR, BS, WIDE), F32),
            pltpu.VMEM((2, 2 * BR, area), BF16),
            pltpu.VMEM((BR, BS, WIDE), F32),
            pltpu.SemaphoreType.DMA((2,)),
        ],
        name="partial",
    )(away, p_rows, *got)
    spread = lax.all_to_all(spread, "row", 0, 0, tiled=True)
    from_next = shift(prev_part, "row", -1)
    from_prev = shift(next_part, "row", 1)
    from_far = shift(far_part, "row", ROWS // 2)

    row_id = jnp.arange(ROWS, dtype=jnp.int32)[:, None]
    source = ((row_id // 2 + 4) % COLS) * BR + jnp.arange(BR, dtype=jnp.int32)[None]
    home = agg_order.reshape(ROWS, 4)
    near = jnp.concatenate([home, home], axis=1)
    choose = near.reshape(-1)[:, None] == source.reshape(-1)[None]
    total = jnp.dot(
        choose.astype(BF16), spread.reshape(ROWS * BR, LANES), preferred_element_type=F32
    )
    high = lax.reduce_precision(total, 8, 7)
    is_low = (jnp.arange(ROWS * BR) % BR // 4 == 1)[:, None]
    back = jnp.where(is_low, total - high, high).astype(BF16).reshape(ROWS, BR, LANES)
    back = lax.all_to_all(back, "row", 0, 0, tiled=True)

    outs = pl.pallas_call(
        product_kernel,
        out_shape=jax.ShapeDtypeStruct((4 * BS, OUTSLOTS * BS), BF16),
        in_specs=[SMEM] + [VMEM] * 7,
        out_specs=VMEM,
        scratch_shapes=[pltpu.VMEM((BR, BS, WIDE), F32)],
        name="product",
    )((row % 2)[None], back, own, from_prev, from_next, from_far, chosen, swapped)
    outs = lax.all_to_all(outs.reshape(COLS, 4 * BS // COLS, OUTSLOTS * BS), "col", 0, 0, tiled=True)

    c_id = jnp.arange(COLS, dtype=jnp.int32)[:, None]
    centre = c_id // 2 + 4 * (c_id % 2)
    j_band = band_columns(2 * BR * section_owner[None] + 2 * centre, agg_order)
    e_id = jnp.arange(2, dtype=jnp.int32)
    j_cross = ((section_owner + 4) % COLS)[None, :, None] * BR + (2 * centre[:, :, None] + e_id) % BR
    j_table = jnp.concatenate([j_band, j_cross], axis=2).reshape(COLS, OUTSLOTS)
    return pl.pallas_call(
        place_kernel,
        out_shape=jax.ShapeDtypeStruct((4 * BS // COLS, NCB * BS), F32),
        in_specs=[SMEM, VMEM],
        out_specs=VMEM,
        scratch_shapes=[pltpu.VMEM((NCB, 4 * BS // COLS, BS), F32)],
        name="place",
    )(j_table, outs)


def solution(mesh):
    in_specs = (
        P("row", "col", None),
        P("row", "col"),
        P("row", "col", None),
        P("row", "col"),
        P(),
        P(),
    )
    out_specs = P(("row", "col"), None)
    return jax.shard_map(inner, mesh=mesh, in_specs=in_specs, out_specs=out_specs, check_vma=False)
```

```python
import jax
import jax.numpy as jnp
from jax import lax
from jax.experimental import pallas as pl
from jax.experimental.pallas import tpu as pltpu
from jax.sharding import PartitionSpec as P

BS = 96
BR = 8
NCB = 64
KK = 4
WIDE = KK * BS
ROWS = 16
COLS = 8
PIECE = BS // ROWS
LANES = PIECE * WIDE
USLOTS = 5
PW = 512
OUTSLOTS = 12
F32 = jnp.float32
BF16 = jnp.bfloat16


def lookup(table, index):
    hit = index[..., None] == jnp.arange(table.shape[0], dtype=jnp.int32)
    return jnp.sum(jnp.where(hit, table, 0), axis=-1)


def shift(value, axis, by):
    size = lax.axis_size(axis)
    return lax.ppermute(value, axis, [(i, (i + by) % size) for i in range(size)])


def band_columns(rows, agg_order):
    center = rows // 2
    places = jnp.stack(
        [(center + NCB - 1) % NCB, center, (center + 1) % NCB, (center + NCB // 2) % NCB], axis=-1
    )
    return lookup(agg_order, places)


def partial_kernel(s_ref, p_ref, *refs):
    got = refs[:COLS]
    x_ref, own_ref, prev_ref, next_ref, far_ref, scr, buf, a_ref, sem = refs[COLS:]
    for sec in range(2):
        for d in range(COLS):

            @pl.when(s_ref[sec] == d)
            def _():
                pltpu.make_async_copy(got[d], buf.at[sec], sem.at[sec]).start()

    for sec in range(2):
        pltpu.make_async_copy(got[0], buf.at[sec], sem.at[sec]).wait()
    for octet in range(BS // 8):
        for sec in range(2):
            rows = []
            for e in range(8):
                at = (octet * 8 + e) * BS
                rows.append(buf[sec, :, at : at + BS].astype(F32))
            turned = jnp.swapaxes(jnp.stack(rows), 0, 1)
            for row in range(2 * BR):
                kk = 2 * sec + row % 2
                a_ref[row // 2, octet * 8 : octet * 8 + 8, kk * BS : (kk + 1) * BS] = turned[row]
    total = [None] * 6
    for i in range(BR):
        q = lax.dot_general(
            p_ref[i], a_ref[i].astype(BF16), (((0,), (0,)), ((), ())), preferred_element_type=F32
        )
        local = i // 2
        for u in range(3):
            w = local + u
            value = q[u * BS : (u + 1) * BS]
            total[w] = value if total[w] is None else total[w] + value
            last = min(local, w) == min(3, w) and i % 2 == 1
            if last and w == 0:
                prev_ref[...] = total[w].astype(BF16)
            elif last and w == 5:
                next_ref[...] = total[w].astype(BF16)
            elif last:
                own_ref[w - 1] = total[w]
        if i % 2 == 0:
            far_ref[local] = q[3 * BS : 4 * BS].astype(BF16)
        scr[i] = q[4 * BS : 5 * BS]
    for octet in range(BS // 8):
        chunk = jnp.swapaxes(scr[:, octet * 8 : octet * 8 + 8, :], 0, 1)
        for e in range(8):
            j, pp = divmod(octet * 8 + e, PIECE)
            x_ref[j, :, pp * WIDE : (pp + 1) * WIDE] = chunk[e].astype(BF16)


def product_kernel(c_ref, r_ref, own_ref, prev_ref, next_ref, far_ref, p_ref, o_ref, near_ref, cross_ref, x_ref, scr):
    for octet in range(BS // 8):
        rows = []
        for e in range(8):
            j, pp = divmod(octet * 8 + e, PIECE)
            rows.append(r_ref[j, :, pp * WIDE : (pp + 1) * WIDE].astype(F32))
        scr[:, octet * 8 : octet * 8 + 8, :] = jnp.swapaxes(jnp.stack(rows), 0, 1)
    for t in range(4):
        g = own_ref[t] + far_ref[t].astype(F32)
        if t == 0:
            g = g + prev_ref[...].astype(F32)
        if t == 3:
            g = g + next_ref[...].astype(F32)
        scr[t] = g + (scr[t] + scr[4 + t])
    for sec in range(2):
        rights = []
        for e in range(2):
            keeper = c_ref[1] == 1
            mine = jnp.where(keeper, p_ref[sec], o_ref[sec])
            theirs = jnp.where(keeper, near_ref[sec], cross_ref[sec])
            rights.append(jnp.where(c_ref[0] == e, mine, theirs)[:, : USLOTS * BS])
        for t in range(4):
            outs = []
            for e in range(2):
                kk = 2 * sec + e
                g = scr[t, :, kk * BS : (kk + 1) * BS]
                high = g.astype(BF16)
                low = (g - high.astype(F32)).astype(BF16)
                out = jnp.dot(high, rights[e], preferred_element_type=F32)
                outs.append(out + jnp.dot(low, rights[e], preferred_element_type=F32))
            span = slice(t * BS, (t + 1) * BS)
            base = sec * OUTSLOTS // 2 * BS
            band = outs[0][:, : 3 * BS] + outs[1][:, : 3 * BS]
            x_ref[span, base : base + 3 * BS] = band.astype(BF16)
            x_ref[span, base + 3 * BS : base + 5 * BS] = outs[0][:, 3 * BS :].astype(BF16)
            x_ref[span, base + 5 * BS : base + 6 * BS] = outs[1][:, 4 * BS :].astype(BF16)


def place_kernel(j_ref, r_ref, out_ref, acc):
    acc[...] = jnp.zeros_like(acc)

    def step(c, carry):
        for s in range(OUTSLOTS):
            at = j_ref[c, s]
            acc[at] += r_ref[c, :, s * BS : (s + 1) * BS].astype(F32)
        return carry

    lax.fori_loop(0, COLS, step, 0)
    for block in range(NCB):
        out_ref[:, block * BS : (block + 1) * BS] = acc[block]


VMEM = pl.BlockSpec(memory_space=pltpu.VMEM)
SMEM = pl.BlockSpec(memory_space=pltpu.SMEM)
ANY = pl.BlockSpec(memory_space=pl.ANY)


def inner(a_blocks, a_mask, p_blocks, p_mask, section_owner, agg_order):
    area = a_blocks.shape[2]
    row, col = lax.axis_index("row"), lax.axis_index("col")
    rows = row * BR + jnp.arange(BR, dtype=jnp.int32)

    band = band_columns(rows, agg_order)
    cross = ((rows // 16 + 4) % COLS) * BR + rows % BR
    live = jnp.stack([jnp.ones_like(rows)] * 3 + [1 - rows % 2], axis=-1) > 0
    fresh = ~jnp.any((band == cross[:, None]) & live, axis=1)
    wanted = jnp.concatenate([band, cross[:, None]], axis=1)
    usable = jnp.concatenate([live, fresh[:, None]], axis=1)
    local = wanted[:, :, None] == col * BR + jnp.arange(BR, dtype=jnp.int32)
    pick = local & usable[:, :, None] & (p_mask[:, None, :] != 0)
    compact = jnp.einsum(
        "iuj,ijf->iuf", pick.astype(BF16), p_blocks, preferred_element_type=F32
    ).astype(BF16)

    sent = lax.all_to_all(compact.reshape(COLS, USLOTS * area // 128, 128), "col", 0, 0, tiled=True)
    line = jnp.arange(COLS * 2 * BR, dtype=jnp.int32)
    heir = (col + line // (2 * BR)) % COLS
    want = (line // 2) % BR * 2 * COLS + 2 * (heir // 2 + 4 * (heir % 2)) + line % 2
    order = jnp.where(want[:, None] == line[None], a_mask.reshape(1, -1), 0)
    tiles = jnp.dot(
        order.astype(BF16), a_blocks.reshape(2 * BR * COLS, area), preferred_element_type=F32
    ).astype(BF16)
    got = []
    for d in range(COLS):
        piece = tiles[2 * BR * d : 2 * BR * (d + 1)]
        got.append(shift(piece, "col", d) if d else piece)
    mine = jnp.sum(sent.astype(F32), axis=0).astype(BF16)
    mine = mine.reshape(USLOTS, BS, BS).transpose(1, 0, 2).reshape(BS, USLOTS * BS)
    mine = jnp.pad(mine, ((0, 0), (0, PW - USLOTS * BS)))
    p_rows = lax.all_to_all(jnp.broadcast_to(mine[None], (COLS, BS, PW)), "col", 0, 0, tiled=True)
    chosen = jnp.stack([mine, mine])
    for bit in range(3):
        moved = lax.ppermute(chosen, "row", [(r, r ^ (2 << bit)) for r in range(ROWS)])
        wrong = (((row // 2) ^ section_owner) >> bit) & 1
        chosen = jnp.where(wrong[:, None, None] == 1, moved, chosen)
    held = [
        (r, c) for r in range(ROWS) for c in range(COLS) if r % 2 == c % 2
    ]
    lent = [
        (r, c) for r in range(ROWS) for c in range(COLS) if r % 2 != c % 2
    ]

    def swap(givers, over_core, over_col):
        pairs = [(r * COLS + c, (r ^ over_core) * COLS + (c ^ over_col)) for r, c in givers]
        return lax.ppermute(chosen, ("row", "col"), pairs)

    swaps = swap(held, 1, 0), swap(lent, 0, 1), swap(lent, 1, 1)

    away = (col - section_owner) % COLS
    spread, own, prev_part, next_part, far_part = pl.pallas_call(
        partial_kernel,
        out_shape=(
            jax.ShapeDtypeStruct((ROWS, BR, LANES), BF16),
            jax.ShapeDtypeStruct((4, BS, WIDE), F32),
            jax.ShapeDtypeStruct((BS, WIDE), BF16),
            jax.ShapeDtypeStruct((BS, WIDE), BF16),
            jax.ShapeDtypeStruct((4, BS, WIDE), BF16),
        ),
        in_specs=[SMEM, VMEM] + [ANY] * COLS,
        out_specs=(VMEM,) * 5,
        scratch_shapes=[
            pltpu.VMEM((BR, BS, WIDE), F32),
            pltpu.VMEM((2, 2 * BR, area), BF16),
            pltpu.VMEM((BR, BS, WIDE), F32),
            pltpu.SemaphoreType.DMA((2,)),
        ],
        name="partial",
    )(away, p_rows, *got)
    spread = lax.all_to_all(spread, "row", 0, 0, tiled=True)
    from_next = shift(prev_part, "row", -1)
    from_prev = shift(next_part, "row", 1)
    from_far = shift(far_part, "row", ROWS // 2)

    row_id = jnp.arange(ROWS, dtype=jnp.int32)[:, None]
    source = ((row_id // 2 + 4) % COLS) * BR + jnp.arange(BR, dtype=jnp.int32)[None]
    home = agg_order.reshape(ROWS, 4)
    near = jnp.concatenate([home, home], axis=1)
    choose = near.reshape(-1)[:, None] == source.reshape(-1)[None]
    total = jnp.dot(
        choose.astype(BF16), spread.reshape(ROWS * BR, LANES), preferred_element_type=F32
    )
    high = lax.reduce_precision(total, 8, 7)
    is_low = (jnp.arange(ROWS * BR) % BR // 4 == 1)[:, None]
    back = jnp.where(is_low, total - high, high).astype(BF16).reshape(ROWS, BR, LANES)
    back = lax.all_to_all(back, "row", 0, 0, tiled=True)

    parity = jnp.stack([col % 2, (row % 2 == col % 2).astype(jnp.int32)])
    outs = pl.pallas_call(
        product_kernel,
        out_shape=jax.ShapeDtypeStruct((4 * BS, OUTSLOTS * BS), BF16),
        in_specs=[SMEM] + [VMEM] * 9,
        out_specs=VMEM,
        scratch_shapes=[
            pltpu.VMEM((BR, BS, WIDE), F32),
        ],
        name="product",
    )(parity, back, own, from_prev, from_next, from_far, chosen, *swaps)
    outs = lax.all_to_all(outs.reshape(COLS, 4 * BS // COLS, OUTSLOTS * BS), "col", 0, 0, tiled=True)

    c_id = jnp.arange(COLS, dtype=jnp.int32)[:, None]
    centre = c_id // 2 + 4 * (c_id % 2)
    j_band = band_columns(2 * BR * section_owner[None] + 2 * centre, agg_order)
    e_id = jnp.arange(2, dtype=jnp.int32)
    j_cross = ((section_owner + 4) % COLS)[None, :, None] * BR + (2 * centre[:, :, None] + e_id) % BR
    j_table = jnp.concatenate([j_band, j_cross], axis=2).reshape(COLS, OUTSLOTS)
    return pl.pallas_call(
        place_kernel,
        out_shape=jax.ShapeDtypeStruct((4 * BS // COLS, NCB * BS), F32),
        in_specs=[SMEM, VMEM],
        out_specs=VMEM,
        scratch_shapes=[pltpu.VMEM((NCB, 4 * BS // COLS, BS), F32)],
        name="place",
    )(j_table, outs)


def solution(mesh):
    in_specs = (
        P("row", "col", None),
        P("row", "col"),
        P("row", "col", None),
        P("row", "col"),
        P(),
        P(),
    )
    out_specs = P(("row", "col"), None)
    return jax.shard_map(inner, mesh=mesh, in_specs=in_specs, out_specs=out_specs, check_vma=False)
```

```python
import jax
import jax.numpy as jnp
from jax import lax
from jax.experimental import pallas as pl
from jax.experimental.pallas import tpu as pltpu
from jax.sharding import PartitionSpec as P

BS = 96
BR = 8
NCB = 64
KK = 4
WIDE = KK * BS
ROWS = 16
COLS = 8
PIECE = BS // ROWS
LANES = PIECE * WIDE
USLOTS = 5
PW = 512
OUTSLOTS = 12
F32 = jnp.float32
BF16 = jnp.bfloat16


def lookup(table, index):
    hit = index[..., None] == jnp.arange(table.shape[0], dtype=jnp.int32)
    return jnp.sum(jnp.where(hit, table, 0), axis=-1)


def shift(value, axis, by):
    size = lax.axis_size(axis)
    return lax.ppermute(value, axis, [(i, (i + by) % size) for i in range(size)])


def band_columns(rows, agg_order):
    center = rows // 2
    places = jnp.stack(
        [(center + NCB - 1) % NCB, center, (center + 1) % NCB, (center + NCB // 2) % NCB], axis=-1
    )
    return lookup(agg_order, places)


def partial_kernel(s_ref, p_ref, *refs):
    got = refs[:COLS]
    x_ref, own_ref, prev_ref, next_ref, far_ref, scr, buf, a_ref, sem = refs[COLS:]
    for sec in range(2):
        for d in range(COLS):

            @pl.when(s_ref[sec] == d)
            def _():
                pltpu.make_async_copy(got[d], buf.at[sec], sem.at[sec]).start()

    for sec in range(2):
        pltpu.make_async_copy(got[0], buf.at[sec], sem.at[sec]).wait()
    for octet in range(BS // 8):
        for sec in range(2):
            rows = []
            for e in range(8):
                at = (octet * 8 + e) * BS
                rows.append(buf[sec, :, at : at + BS].astype(F32))
            turned = jnp.swapaxes(jnp.stack(rows), 0, 1)
            for row in range(2 * BR):
                kk = 2 * sec + row % 2
                a_ref[row // 2, octet * 8 : octet * 8 + 8, kk * BS : (kk + 1) * BS] = turned[row]
    total = [None] * 6
    for i in range(BR):
        q = lax.dot_general(
            p_ref[i], a_ref[i].astype(BF16), (((0,), (0,)), ((), ())), preferred_element_type=F32
        )
        local = i // 2
        for u in range(3):
            w = local + u
            value = q[u * BS : (u + 1) * BS]
            total[w] = value if total[w] is None else total[w] + value
            last = min(local, w) == min(3, w) and i % 2 == 1
            if last and w == 0:
                prev_ref[...] = total[w].astype(BF16)
            elif last and w == 5:
                next_ref[...] = total[w].astype(BF16)
            elif last:
                own_ref[w - 1] = total[w]
        if i % 2 == 0:
            far_ref[local] = q[3 * BS : 4 * BS].astype(BF16)
        scr[i] = q[4 * BS : 5 * BS]
    for octet in range(BS // 8):
        chunk = jnp.swapaxes(scr[:, octet * 8 : octet * 8 + 8, :], 0, 1)
        for e in range(8):
            j, pp = divmod(octet * 8 + e, PIECE)
            x_ref[j, :, pp * WIDE : (pp + 1) * WIDE] = chunk[e].astype(BF16)


def product_kernel(c_ref, r_ref, own_ref, prev_ref, next_ref, far_ref, p_ref, o_ref, near_ref, cross_ref, x_ref, scr):
    for octet in range(BS // 8):
        rows = []
        for e in range(8):
            j, pp = divmod(octet * 8 + e, PIECE)
            rows.append(r_ref[j, :, pp * WIDE : (pp + 1) * WIDE].astype(F32))
        scr[:, octet * 8 : octet * 8 + 8, :] = jnp.swapaxes(jnp.stack(rows), 0, 1)
    for t in range(4):
        g = own_ref[t] + far_ref[t].astype(F32)
        if t == 0:
            g = g + prev_ref[...].astype(F32)
        if t == 3:
            g = g + next_ref[...].astype(F32)
        scr[t] = g + (scr[t] + scr[4 + t])
    for sec in range(2):
        rights = []
        for e in range(2):
            keeper = c_ref[1] == 1
            mine = jnp.where(keeper, p_ref[sec], o_ref[sec])
            theirs = jnp.where(keeper, near_ref[sec], cross_ref[sec])
            rights.append(jnp.where(c_ref[0] == e, mine, theirs)[:, : USLOTS * BS])
        for t in range(4):
            outs = []
            for e in range(2):
                kk = 2 * sec + e
                g = scr[t, :, kk * BS : (kk + 1) * BS]
                high = g.astype(BF16)
                low = (g - high.astype(F32)).astype(BF16)
                out = jnp.dot(high, rights[e], preferred_element_type=F32)
                outs.append(out + jnp.dot(low, rights[e], preferred_element_type=F32))
            span = slice(t * BS, (t + 1) * BS)
            base = sec * OUTSLOTS // 2 * BS
            band = outs[0][:, : 3 * BS] + outs[1][:, : 3 * BS]
            x_ref[span, base : base + 3 * BS] = band.astype(BF16)
            x_ref[span, base + 3 * BS : base + 5 * BS] = outs[0][:, 3 * BS :].astype(BF16)
            x_ref[span, base + 5 * BS : base + 6 * BS] = outs[1][:, 4 * BS :].astype(BF16)


def place_kernel(j_ref, r_ref, out_ref, acc, whole, sem):
    acc[...] = jnp.zeros_like(acc)

    def step(c, carry):
        for s in range(OUTSLOTS):
            at = j_ref[c, s]
            acc[at] += r_ref[c, :, s * BS : (s + 1) * BS].astype(F32)
        return carry

    lax.fori_loop(0, COLS, step, 0)
    span = NCB // 4 * BS
    copies = []
    for part in range(4):
        for block in range(part * NCB // 4, (part + 1) * NCB // 4):
            whole[:, block * BS : (block + 1) * BS] = acc[block]
        at = slice(part * span, (part + 1) * span)
        copies.append(pltpu.make_async_copy(whole.at[:, at], out_ref.at[:, at], sem.at[part]))
        copies[part].start()
    for copy in copies:
        copy.wait()


VMEM = pl.BlockSpec(memory_space=pltpu.VMEM)
SMEM = pl.BlockSpec(memory_space=pltpu.SMEM)
ANY = pl.BlockSpec(memory_space=pl.ANY)


def inner(a_blocks, a_mask, p_blocks, p_mask, section_owner, agg_order):
    area = a_blocks.shape[2]
    row, col = lax.axis_index("row"), lax.axis_index("col")
    rows = row * BR + jnp.arange(BR, dtype=jnp.int32)

    band = band_columns(rows, agg_order)
    cross = ((rows // 16 + 4) % COLS) * BR + rows % BR
    live = jnp.stack([jnp.ones_like(rows)] * 3 + [1 - rows % 2], axis=-1) > 0
    fresh = ~jnp.any((band == cross[:, None]) & live, axis=1)
    wanted = jnp.concatenate([band, cross[:, None]], axis=1)
    usable = jnp.concatenate([live, fresh[:, None]], axis=1)
    local = wanted[:, :, None] == col * BR + jnp.arange(BR, dtype=jnp.int32)
    pick = local & usable[:, :, None] & (p_mask[:, None, :] != 0)
    compact = jnp.einsum(
        "iuj,ijf->iuf", pick.astype(BF16), p_blocks, preferred_element_type=F32
    ).astype(BF16)

    sent = lax.all_to_all(compact.reshape(COLS, USLOTS * area // 128, 128), "col", 0, 0, tiled=True)
    line = jnp.arange(COLS * 2 * BR, dtype=jnp.int32)
    heir = (col + line // (2 * BR)) % COLS
    want = (line // 2) % BR * 2 * COLS + 2 * (heir // 2 + 4 * (heir % 2)) + line % 2
    order = jnp.where(want[:, None] == line[None], a_mask.reshape(1, -1), 0)
    tiles = jnp.dot(
        order.astype(BF16), a_blocks.reshape(2 * BR * COLS, area), preferred_element_type=F32
    ).astype(BF16)
    got = []
    for d in range(COLS):
        piece = tiles[2 * BR * d : 2 * BR * (d + 1)]
        got.append(shift(piece, "col", d) if d else piece)
    mine = jnp.sum(sent.astype(F32), axis=0).astype(BF16)
    mine = mine.reshape(USLOTS, BS, BS).transpose(1, 0, 2).reshape(BS, USLOTS * BS)
    mine = jnp.pad(mine, ((0, 0), (0, PW - USLOTS * BS)))
    p_rows = lax.all_to_all(jnp.broadcast_to(mine[None], (COLS, BS, PW)), "col", 0, 0, tiled=True)
    chosen = jnp.stack([mine, mine])
    for bit in range(3):
        moved = lax.ppermute(chosen, "row", [(r, r ^ (2 << bit)) for r in range(ROWS)])
        wrong = (((row // 2) ^ section_owner) >> bit) & 1
        chosen = jnp.where(wrong[:, None, None] == 1, moved, chosen)
    held = [
        (r, c) for r in range(ROWS) for c in range(COLS) if r % 2 == c % 2
    ]
    lent = [
        (r, c) for r in range(ROWS) for c in range(COLS) if r % 2 != c % 2
    ]

    def swap(givers, over_core, over_col):
        pairs = [(r * COLS + c, (r ^ over_core) * COLS + (c ^ over_col)) for r, c in givers]
        return lax.ppermute(chosen, ("row", "col"), pairs)

    swaps = swap(held, 1, 0), swap(lent, 0, 1), swap(lent, 1, 1)

    away = (col - section_owner) % COLS
    spread, own, prev_part, next_part, far_part = pl.pallas_call(
        partial_kernel,
        out_shape=(
            jax.ShapeDtypeStruct((ROWS, BR, LANES), BF16),
            jax.ShapeDtypeStruct((4, BS, WIDE), F32),
            jax.ShapeDtypeStruct((BS, WIDE), BF16),
            jax.ShapeDtypeStruct((BS, WIDE), BF16),
            jax.ShapeDtypeStruct((4, BS, WIDE), BF16),
        ),
        in_specs=[SMEM, VMEM] + [ANY] * COLS,
        out_specs=(VMEM,) * 5,
        scratch_shapes=[
            pltpu.VMEM((BR, BS, WIDE), F32),
            pltpu.VMEM((2, 2 * BR, area), BF16),
            pltpu.VMEM((BR, BS, WIDE), F32),
            pltpu.SemaphoreType.DMA((2,)),
        ],
        name="partial",
    )(away, p_rows, *got)
    spread = lax.all_to_all(spread, "row", 0, 0, tiled=True)
    from_next = shift(prev_part, "row", -1)
    from_prev = shift(next_part, "row", 1)
    from_far = shift(far_part, "row", ROWS // 2)

    row_id = jnp.arange(ROWS, dtype=jnp.int32)[:, None]
    source = ((row_id // 2 + 4) % COLS) * BR + jnp.arange(BR, dtype=jnp.int32)[None]
    home = agg_order.reshape(ROWS, 4)
    near = jnp.concatenate([home, home], axis=1)
    choose = near.reshape(-1)[:, None] == source.reshape(-1)[None]
    total = jnp.dot(
        choose.astype(BF16), spread.reshape(ROWS * BR, LANES), preferred_element_type=F32
    )
    high = lax.reduce_precision(total, 8, 7)
    is_low = (jnp.arange(ROWS * BR) % BR // 4 == 1)[:, None]
    back = jnp.where(is_low, total - high, high).astype(BF16).reshape(ROWS, BR, LANES)
    back = lax.all_to_all(back, "row", 0, 0, tiled=True)

    parity = jnp.stack([col % 2, (row % 2 == col % 2).astype(jnp.int32)])
    outs = pl.pallas_call(
        product_kernel,
        out_shape=jax.ShapeDtypeStruct((4 * BS, OUTSLOTS * BS), BF16),
        in_specs=[SMEM] + [VMEM] * 9,
        out_specs=VMEM,
        scratch_shapes=[
            pltpu.VMEM((BR, BS, WIDE), F32),
        ],
        name="product",
    )(parity, back, own, from_prev, from_next, from_far, chosen, *swaps)
    outs = lax.all_to_all(outs.reshape(COLS, 4 * BS // COLS, OUTSLOTS * BS), "col", 0, 0, tiled=True)

    c_id = jnp.arange(COLS, dtype=jnp.int32)[:, None]
    centre = c_id // 2 + 4 * (c_id % 2)
    j_band = band_columns(2 * BR * section_owner[None] + 2 * centre, agg_order)
    e_id = jnp.arange(2, dtype=jnp.int32)
    j_cross = ((section_owner + 4) % COLS)[None, :, None] * BR + (2 * centre[:, :, None] + e_id) % BR
    j_table = jnp.concatenate([j_band, j_cross], axis=2).reshape(COLS, OUTSLOTS)
    return pl.pallas_call(
        place_kernel,
        out_shape=jax.ShapeDtypeStruct((4 * BS // COLS, NCB * BS), F32),
        in_specs=[SMEM, VMEM],
        out_specs=ANY,
        scratch_shapes=[
            pltpu.VMEM((NCB, 4 * BS // COLS, BS), F32),
            pltpu.VMEM((4 * BS // COLS, NCB * BS), F32),
            pltpu.SemaphoreType.DMA((4,)),
        ],
        compiler_params=pltpu.CompilerParams(vmem_limit_bytes=16 << 20),
        name="place",
    )(j_table, outs)


def solution(mesh):
    in_specs = (
        P("row", "col", None),
        P("row", "col"),
        P("row", "col", None),
        P("row", "col"),
        P(),
        P(),
    )
    out_specs = P(("row", "col"), None)
    return jax.shard_map(inner, mesh=mesh, in_specs=in_specs, out_specs=out_specs, check_vma=False)
```
